32 devices in a mesh: seq: 8 (over z, y), head: 4 (over x, core).
Axes of the slice: x: 2, y: 2, z: 4, core: 2. Of those that a mesh axis runs over, the one named last changes fastest.
Arguments:
- queries: bfloat16 [8192, 1024], P('seq', 'head'), may hold values from -6 to 6
- keys_values: bfloat16 [8192, 128], P('seq'), may hold values from -6 to 6
- init_state: float32 [64, 2080], replicated, may hold values from -48 to 48
- out_grad: bfloat16 [8192, 1024], P('seq', 'head'), may hold values from -6 to 6
Outputs:
- attended: bfloat16 [8192, 1024], P('seq', 'head')
- query_grad: bfloat16 [8192, 1024], P('seq', 'head')
- kv_grad: float32 [8192, 128], P('seq')
- init_grad: float32 [64, 2080], P(None, 'head')
The draws below stay inside these ranges and needn't reach their ends.
All inputs are finite; a program needn't handle non-finite values.
Results may differ from the reference program's by a relative error of at most 0.0071.
Values sent between devices are 32-bit elements; how exact they have to be, the bound alone decides.
A program may use at most 128 MiB of HBM per device.

```python
import jax
import jax.numpy as jnp
import numpy as np
from jax import lax

HEADS = 16
HEAD_DIM = 64
FEATURES = 2080
GROUP = 1024
TOKENS = 8192


def steps_of(rng, dims, shards, least, high):
    level, own = 1.0, jax.random.fold_in(rng, 6)
    for axis_at, blocks in shards:
        steps = jnp.exp(jax.random.uniform(jax.random.fold_in(own, axis_at), (blocks,), jnp.float32, least / len(shards), high / len(shards)))
        level = level * jnp.repeat(steps, dims[axis_at] // blocks).reshape([-1 if axis == axis_at else 1 for axis in range(len(dims))])
    return level


def bell_draw(key, dims, spread, bound, cuts=(), kind=jnp.bfloat16):
    values = spread * jax.random.normal(key, dims, jnp.float32)
    if cuts:
        values = values * steps_of(key, dims, cuts, -0.22, 0.18)
    return jnp.clip(values, -bound, bound).astype(kind)


def setup_inputs(seed: int = 0) -> dict:
    key_of = jax.random.split(jax.random.key(seed), 5)
    return {
        "queries": bell_draw(key_of[0], (TOKENS, HEADS * HEAD_DIM), 1.0, 6.0, ((0, 8), (1, 4))),
        "keys_values": bell_draw(key_of[1], (TOKENS, 2 * HEAD_DIM), 1.0, 6.0, ((0, 8),)),
        "init_state": bell_draw(key_of[2], (HEAD_DIM, FEATURES), 8.0, 48.0, (), jnp.float32),
        "out_grad": bell_draw(key_of[3], (TOKENS, HEADS * HEAD_DIM), 1.0, 6.0, ((0, 8), (1, 4))),
    }


epsilon = 1e-06

def pair_tables(width):
    left_index, right_index = np.triu_indices(width)
    factor = np.where(left_index == right_index, 1.0, np.sqrt(2.0)) / np.sqrt(width)
    return (jnp.asarray(left_index, jnp.int32), jnp.asarray(right_index, jnp.int32), jnp.asarray(factor, jnp.float32))

def product(first, second, contract):
    return lax.dot_general(first.astype(jnp.float32), second.astype(jnp.float32), (contract, ((), ())), precision=lax.Precision.HIGHEST, preferred_element_type=jnp.float32)

def features(wide, tables):
    left_index, right_index, factor = tables
    return jnp.take(wide, left_index, axis=1) * jnp.take(wide, right_index, axis=1) * factor

def feature_grad(rows_in, upstream, tables):
    _, pullback = jax.vjp(lambda inner: features(inner, tables), rows_in.astype(jnp.float32))
    return pullback(lax.optimization_barrier(upstream).astype(jnp.float32))[0]

def head_pass(query, keys, values, start_low, grad, tables):
    width = query.shape[1]
    length = query.shape[0]
    qfeat = features(query.astype(jnp.float32), tables).astype(jnp.bfloat16)
    inter = product(qfeat, start_low, ((1,), (1,)))
    logits = product(query, keys, ((1,), (1,)))
    causal = lax.broadcasted_iota(jnp.int32, (length, length), 0) >= lax.broadcasted_iota(jnp.int32, (length, length), 1)
    weights = jnp.where(causal, logits * logits / width, 0.0).astype(jnp.bfloat16)
    numer = inter + product(weights, values, ((1,), (0,)))
    scale = lax.rsqrt(lax.optimization_barrier(jnp.mean(numer * numer, axis=1, keepdims=True)) + epsilon)
    normed = numer * scale
    upstream = grad.astype(jnp.float32)
    d_numer = (scale * (upstream - normed * lax.optimization_barrier(jnp.mean(upstream * normed, axis=1, keepdims=True)))).astype(jnp.bfloat16)
    d_qfeat = product(d_numer, start_low, ((1,), (0,))).astype(jnp.bfloat16)
    d_weights = product(d_numer, values, ((1,), (1,)))
    d_logits = jnp.where(causal, d_weights * logits * (2.0 / width), 0.0).astype(jnp.bfloat16)
    query_total = feature_grad(query, d_qfeat, tables) + product(d_logits, keys, ((1,), (0,)))
    key_local = product(d_logits, query, ((0,), (0,)))
    value_local = product(weights, d_numer, ((0,), (0,)))
    state_local = product(d_numer, qfeat, ((0,), (0,)))
    return (normed.astype(jnp.bfloat16), query_total.astype(jnp.bfloat16), key_local, value_local, state_local)

def reference(queries, keys_values, init_state, out_grad):
    tables = pair_tables(HEAD_DIM)
    count = TOKENS // GROUP
    query_blocks = queries.reshape(count, GROUP, HEADS * HEAD_DIM)
    kv_blocks = keys_values.reshape(count, GROUP, 2 * HEAD_DIM)
    grad_blocks = out_grad.reshape(count, GROUP, HEADS * HEAD_DIM)

    def block_update(block):
        kfeat = features(block[:, :HEAD_DIM].astype(jnp.float32), tables).astype(jnp.bfloat16)
        return product(block[:, HEAD_DIM:], kfeat, ((0,), (0,)))
    updates = lax.map(block_update, kv_blocks)
    before = jnp.concatenate([jnp.zeros_like(updates[:1]), jnp.cumsum(updates[:-1], axis=0)], axis=0)
    starts = (init_state[None] + before).astype(jnp.bfloat16)

    def block_pass(inputs):
        query_block, kv_block, grad_block, start_low = inputs
        keys = kv_block[:, :HEAD_DIM]
        values = kv_block[:, HEAD_DIM:]
        query_heads = query_block.reshape(GROUP, HEADS, HEAD_DIM).transpose(1, 0, 2)
        grad_heads = grad_block.reshape(GROUP, HEADS, HEAD_DIM).transpose(1, 0, 2)

        def one_head(pair):
            return head_pass(pair[0], keys, values, start_low, pair[1], tables)
        normed, qgrad, key_part, value_part, state_part = lax.map(one_head, (query_heads, grad_heads))
        return (normed.transpose(1, 0, 2).reshape(GROUP, HEADS * HEAD_DIM), qgrad.transpose(1, 0, 2).reshape(GROUP, HEADS * HEAD_DIM), lax.optimization_barrier(jnp.sum(key_part, axis=0)), lax.optimization_barrier(jnp.sum(value_part, axis=0)), lax.optimization_barrier(jnp.sum(state_part, axis=0)))
    attended, query_grad, key_local, value_local, state_grads = lax.map(block_pass, (query_blocks, kv_blocks, grad_blocks, starts))
    suffix = jnp.cumsum(state_grads[::-1], axis=0)[::-1]
    later = jnp.concatenate([suffix[1:], jnp.zeros_like(suffix[:1])], axis=0).astype(jnp.bfloat16)
    init_grad = suffix[0]

    def key_pass(inputs):
        kv_block, later_low = inputs
        keys = kv_block[:, :HEAD_DIM]
        values = kv_block[:, HEAD_DIM:]
        kfeat = features(keys.astype(jnp.float32), tables).astype(jnp.bfloat16)
        value_state = product(kfeat, later_low, ((1,), (1,)))
        d_kfeat = product(values, later_low, ((1,), (0,))).astype(jnp.bfloat16)
        key_state = feature_grad(keys, d_kfeat, tables)
        return (key_state, value_state)
    key_state, value_state = lax.map(key_pass, (kv_blocks, later))
    kv_grad = jnp.concatenate([key_local + key_state, value_local + value_state], axis=2)
    return (attended.reshape(TOKENS, HEADS * HEAD_DIM), query_grad.reshape(TOKENS, HEADS * HEAD_DIM), kv_grad.reshape(TOKENS, 2 * HEAD_DIM).astype(jnp.float32), init_grad)
```

```python
import functools

import jax
import jax.numpy as jnp
import numpy as np
from jax import lax
from jax.experimental import pallas as pl
from jax.experimental.pallas import tpu as pltpu
from jax.sharding import PartitionSpec as P

HEAD_DIM = 64
GROUP = 1024
EPS = 1e-06
CHUNK = 256
MESH = pl.DeviceIdType.MESH
F32, BF16 = jnp.float32, jnp.bfloat16


def padded_layout(width):
    starts, at = [], 0
    for a in range(width):
        starts.append(at)
        at += width - a // 8 * 8
    return starts, at


STARTS, PADDED = padded_layout(HEAD_DIM)
CANON = [a * HEAD_DIM - a * (a - 1) // 2 for a in range(HEAD_DIM)]


def dot(first, second, contract=((1,), (0,))):
    return lax.dot_general(first, second, (contract, ((), ())), preferred_element_type=F32)


def edge_weights(cols):
    row = lax.broadcasted_iota(jnp.int32, (8, cols), 0)
    return [
        jnp.where(row < m, 0.0, jnp.where(row == m, float(np.sqrt(0.5)), 1.0)).astype(F32)
        for m in range(8)
    ]


def write_features(x_ref, xs_ref, f_ref, cols):
    edges = edge_weights(cols)
    for a in range(0, HEAD_DIM, 2):
        base = a // 8 * 8
        parts = []
        for c in (a, a + 1):
            prod = x_ref[c : c + 1, :] * xs_ref[base:, :]
            parts.append(prod[:8] * edges[c % 8])
            if base + 8 < HEAD_DIM:
                parts.append(prod[8:])
        at = STARTS[a]
        f_ref[at : at + 2 * (HEAD_DIM - base), :] = jnp.concatenate(parts, axis=0).astype(BF16)


def feature_grad(xs_ref, df_ref, row_ref, cols):
    edges = edge_weights(cols)
    tiles = HEAD_DIM // 8
    acc = [jnp.zeros((8, cols), F32) for _ in range(tiles)]
    for a in range(HEAD_DIM):
        first = a // 8
        xa = jnp.broadcast_to(xs_ref[a : a + 1, :], (8, cols))
        total = None
        for t in range(first, tiles):
            at = STARTS[a] + (t - first) * 8
            part = df_ref[at : at + 8, :]
            if t == first:
                part = part * edges[a % 8]
            acc[t] = acc[t] + part * xa
            term = part * xs_ref[t * 8 : t * 8 + 8, :]
            total = term if total is None else total + term
        row_ref[a : a + 1, :] = jnp.sum(total, axis=0, keepdims=True)
    return jnp.concatenate(acc, axis=0) + row_ref[...]


def scaled(x):
    return x * float(np.sqrt(2.0 / HEAD_DIM))


def places(ns, nh):
    s, h = lax.axis_index("seq"), lax.axis_index("head")
    groups = ns // 2
    g, p = s // 2, s % 2
    beside = h + 1 - 2 * (h % 2)
    partner = (s + 1 - 2 * p, h)
    ring = [(lax.rem(g + k, groups) * 2 + p, h) for k in range(1, groups)]
    across = [(s, lax.rem(h + k, nh)) for k in range(1, nh)]
    return s, h, g, p, beside, partner, ring, across


def block(index, size):
    return pl.ds(pl.multiple_of(index * size, 8), size)


class Links:
    def __init__(self, sends, recvs):
        self.sends, self.recvs, self.used = sends, recvs, 0

    def copy(self, src, dst, device):
        k = self.used
        self.used += 1
        return pltpu.make_async_remote_copy(
            src_ref=src, dst_ref=dst, send_sem=self.sends.at[k], recv_sem=self.recvs.at[k],
            device_id=device, device_id_type=MESH,
        )


def gather_copies(links, nh, s, h, beside, src, out, size, spot):
    far = []
    for k in range(2, nh, 2):
        to = lax.rem(h + k, nh)
        first = links.copy(src, out.at[spot(h)], (s, to))
        came = out.at[spot(lax.rem(h + nh - k, nh))]
        far.append((first, links.copy(came, came, (s, beside))))
    near = links.copy(src, out.at[spot(h)], (s, beside))
    return far, near


def spread_piece(links, nh, s, h, beside, out, half, slot):
    spot = lambda owner: block(owner * 2 + slot, half)
    return gather_copies(links, nh, s, h, beside, out.at[spot(h)], out, half, spot)


def start_gather(gather):
    far, near = gather
    for first, _ in far:
        first.start()
    near.start()


def forward_gather(gather):
    for first, second in gather[0]:
        first.wait_recv()
        second.start()


def finish_gather(gather):
    far, near = gather
    for first, second in far:
        first.wait_send()
        second.wait()
    near.wait()


def padded_column(c):
    a = max(a for a in range(HEAD_DIM) if CANON[a] <= c)
    return STARTS[a] + a % 8 + c - CANON[a]


def windows(features, nh):
    wide = features // nh
    ends = [(padded_column(k * wide), padded_column(k * wide + wide - 1)) for k in range(nh)]
    width = max(-(-(hi + 1) // 128) * 128 - lo // 128 * 128 for lo, hi in ends)
    return [min(lo // 128 * 128, PADDED - width) for lo, _ in ends], width


def window_at(starts, owner, nh):
    at = starts[0]
    for k in range(1, nh):
        at = at + (starts[k] - starts[k - 1]) * ((owner + nh - k) // nh)
    return at


def masked(full, causal):
    n = full.shape[0]
    last = jnp.where(causal, full[n - CHUNK :], 0.0)
    if n == CHUNK:
        return last.astype(BF16)
    return jnp.concatenate([full[: n - CHUNK], last], axis=0).astype(BF16)


def main_kernel(ns, nh, names, starts, width, *refs):
    r = dict(zip(names, refs))
    q_ref, kv_ref, init_ref, og_ref = r["q"], r["kv"], r["init"], r["og"]
    kvt, xs, x, row, df, f_all = r["kvt"], r["xs"], r["x"], r["row"], r["df"], r["f"]
    qt, ogt, attt, qgt, dnt = r["qt"], r["ogt"], r["attt"], r["qgt"], r["dnt"]
    start, startt, keys, vals, kt, vt = (
        r["start"], r["startt"], r["keys"], r["vals"], r["kt"], r["vt"]
    )
    carry, later_ref, sg, kvl = r["carry"], r["later"], r["sg"], r["kvl"]
    padt, tall = r["padt"], r["tall"]
    tokens = q_ref.shape[0]
    heads = q_ref.shape[1] // HEAD_DIM
    chunks = tokens // CHUNK
    features = init_ref.shape[1]
    rows, quarter, half, groups = HEAD_DIM // nh, tokens // nh, HEAD_DIM // nh // 2, ns // 2
    s, h, g, p, beside, partner, ring, across = places(ns, nh)
    links = Links(r["sends"], r["recvs"])
    barrier = pltpu.get_barrier_semaphore()
    for device in [partner] + ring + across:
        pl.semaphore_signal(barrier, inc=1, device_id=device, device_id_type=MESH)

    kvt[...] = kv_ref[...].astype(F32).T
    mine_vals = kvt[block(HEAD_DIM // rows + h, rows), :].astype(BF16)
    u_ref = r["u"]
    for c in range(chunks):
        at = slice(c * CHUNK, (c + 1) * CHUNK)
        xk = kvt.at[:HEAD_DIM, at]
        xs[...] = scaled(xk[...])
        write_features(xk, xs, f_all.at[c], CHUNK)
        part = dot(mine_vals[:, at], f_all[c], ((1,), (1,)))
        if c == 0:
            u_ref[...] = part
        else:
            u_ref[...] += part
    pl.semaphore_wait(barrier, 1 + len(ring) + len(across))
    pair = r["pair"]
    swap = links.copy(u_ref.at[block(1 - p, half), :], pair, partner)
    swap.start()

    qt[...] = q_ref[...].astype(F32).T
    kt[...] = kvt[:HEAD_DIM, :].astype(BF16)
    vt[...] = kvt[HEAD_DIM:, :].astype(BF16)
    keys[...] = kv_ref[:, :HEAD_DIM]
    vals[...] = kv_ref[:, HEAD_DIM:]
    causal = lax.broadcasted_iota(jnp.int32, (CHUNK, CHUNK), 0) <= lax.broadcasted_iota(
        jnp.int32, (CHUNK, CHUNK), 1
    )

    def inner(c):
        n = (c + 1) * CHUNK
        at = slice(c * CHUNK, n)

        def one_head(k, _):
            here = pl.ds(pl.multiple_of(k * HEAD_DIM, HEAD_DIM), HEAD_DIM)
            query = qt[here, at]
            x[...] = query
            xs[...] = scaled(query)
            write_features(x, xs, f_all.at[c * heads + k], CHUNK)
            logits = dot(keys[:n], query.astype(BF16))
            weights = masked(logits * logits * (1.0 / HEAD_DIM), causal)
            r[f"logits{c}"][k] = logits
            r[f"weights{c}"][k] = weights
            attt[here, at] = dot(vt[:, :n], weights)
            return 0

        lax.fori_loop(0, heads, one_head, 0)

    def upward(c):
        n = (c + 1) * CHUNK
        at = slice(c * CHUNK, n)

        def one_head(k, _):
            here = pl.ds(pl.multiple_of(k * HEAD_DIM, HEAD_DIM), HEAD_DIM)
            query = qt[here, at]
            xs[...] = scaled(query)
            dn = dnt[here, at]
            df[...] = dot(startt[...], dn)
            dw = dot(vals[:n], dn)
            dl = masked(dw * r[f"logits{c}"][k] * (2.0 / HEAD_DIM), causal)
            qgt[here, at] = dot(kt[:, :n], dl) + feature_grad(xs, df, row, CHUNK)
            kvl[:n, :HEAD_DIM] += dot(dl, query.astype(BF16), ((1,), (1,)))
            kvl[:n, HEAD_DIM:] += dot(r[f"weights{c}"][k], dn, ((1,), (1,)))
            return 0

        lax.fori_loop(0, heads, one_head, 0, unroll=True)

    wide = r["wide"]
    whole_lanes = features // 128 * 128
    padt[...] = jnp.zeros_like(padt)
    wide[:, whole_lanes:] = jnp.zeros_like(wide[:, whole_lanes:])
    wide[:, :features] = init_ref[...]
    tall[...] = wide[...].T
    for a in range(HEAD_DIM):
        at = STARTS[a] + a % 8
        padt[at : at + HEAD_DIM - a, :] = tall[CANON[a] : CANON[a] + HEAD_DIM - a, :]
    r["initp"][...] = padt[...].T
    ogt[...] = og_ref[...].astype(F32).T
    swap.wait()
    both = r["both"]
    mine = u_ref[block(p, half), :]
    both[...] = mine + pair[...]
    moves = [links.copy(both, r["got"].at[k], ring[k]) for k in range(groups - 1)]
    for k, move in enumerate(moves):
        @pl.when(g + k + 1 < groups)
        def _(move=move):
            move.start()
    order = list(range(chunks))
    inner(order[-1])
    for c in order[:-3]:
        inner(c)
    ours = block(h * 2 + p, half)
    mate = r["mate"]
    base, mated = jnp.where(p == 1, pair[...], 0.0), jnp.where(p == 0, mine, 0.0)
    carry[ours, :] = base
    mate[...] = mated
    for k, move in enumerate(moves):
        @pl.when(g - k - 1 >= 0)
        def _(move=move, k=k):
            move.wait_recv()
            carry[ours, :] += r["got"][k]
            mate[...] += r["got"][k]
    back = links.copy(mate, carry.at[ours, :], partner)
    back.start()
    own_half = spread_piece(links, nh, s, h, beside, carry, half, p)
    start_gather(own_half)
    inner(order[-3])
    other_half = spread_piece(links, nh, s, h, beside, carry, half, 1 - p)
    back.wait_recv()
    start_gather(other_half)
    forward_gather(own_half)
    inner(order[-2])
    forward_gather(other_half)

    for k, move in enumerate(moves):
        @pl.when(g + k + 1 < groups)
        def _(move=move):
            move.wait_send()
    back.wait_send()
    finish_gather(own_half)
    finish_gather(other_half)
    first_state = r["initp"][...] + carry[...]
    start[...] = first_state.astype(BF16)
    startt[...] = first_state.T.astype(BF16)


    def normalize(c, _):
        at = pl.ds(pl.multiple_of(c * CHUNK, CHUNK), CHUNK)
        for k in range(heads):
            here = slice(k * HEAD_DIM, (k + 1) * HEAD_DIM)
            numer = attt[here, at] + dot(start[...], f_all[c * heads + k])
            scale = lax.rsqrt(jnp.mean(numer * numer, axis=0, keepdims=True) + EPS)
            normed = numer * scale
            up = ogt[here, at]
            attt[here, at] = normed
            dn = (scale * (up - normed * jnp.mean(up * normed, axis=0, keepdims=True))).astype(BF16)
            dnt[here, at] = dn
        return 0

    lax.fori_loop(0, chunks, normalize, 0, unroll=True)

    def state_columns(t, _):
        cols = pl.ds(pl.multiple_of(t * CHUNK, CHUNK), CHUNK)
        sg[:, cols] = sum(
            dot(
                dnt[k * HEAD_DIM : (k + 1) * HEAD_DIM, c * CHUNK : (c + 1) * CHUNK],
                f_all[c * heads + k, cols, :],
                ((1,), (1,)),
            )
            for c in range(chunks)
            for k in range(heads)
        )
        return 0

    lax.fori_loop(0, PADDED // CHUNK, state_columns, 0, unroll=3)

    near, far, mid, own = r["near"], r["far"], r["mid"], r["own"]
    evens = range(2, nh + 1, 2)
    first, second = [], []
    for i, k in enumerate(evens):
        src = sg.at[block(lax.rem(beside + k, nh), rows), :]
        first.append(links.copy(src, near.at[i], (s, beside)))
        first[-1].start()
    kvl[...] = jnp.zeros_like(kvl)
    upward(0)
    for i, k in enumerate(evens):
        first[i].wait_recv()
        summed = sg[block(lax.rem(h + k, nh), rows), :] + near[i]
        if k == nh:
            own[...] = summed
        else:
            mid[i] = summed
            second.append(links.copy(mid.at[i], far.at[i], (s, lax.rem(h + k, nh))))
            second[-1].start()
    for c in order[1:-2]:
        upward(c)
    for i, copy in enumerate(second):
        copy.wait_recv()
        own[...] += far[i]
    spair, sboth = r["spair"], r["sboth"]
    sswap = links.copy(own.at[block(1 - p, half), :], spair, partner)
    sswap.start()
    att_ref, qg_ref = r["att"], r["qg"]
    upward(order[-2])
    sswap.wait()
    mine = own[block(p, half), :]
    sboth[...] = mine + spair[...]
    smoves = [links.copy(sboth, r["sgot"].at[k], ring[k]) for k in range(groups - 1)]
    for move in smoves:
        move.start()
    upward(order[-1])
    kvnear, kvfar, kvmid = r["kvnear"], r["kvfar"], r["kvmid"]
    kvfirst, kvsecond = [], []
    for i, k in enumerate(evens):
        src = kvl.at[block(lax.rem(beside + k, nh), quarter), :]
        kvfirst.append(links.copy(src, kvnear.at[i], (s, beside)))
        kvfirst[-1].start()
    smate, tot, total_ref = r["smate"], r["tot"], r["total"]
    later = jnp.where(p == 0, spair[...], 0.0)
    mated = jnp.where(p == 1, mine, 0.0)
    whole = sboth[...]
    for k, move in enumerate(smoves):
        move.wait_recv()
        whole = whole + r["sgot"][k]
        after = jnp.where(k + 1 > g, r["sgot"][k], 0.0)
        later = later + after
        mated = mated + after
    later_ref[ours, :] = later
    smate[...] = mated
    tot[...] = whole
    sback = links.copy(smate, later_ref.at[ours, :], partner)
    sback.start()
    own_half = spread_piece(links, nh, s, h, beside, later_ref, half, p)
    start_gather(own_half)
    total_swap = links.copy(tot, total_ref.at[block(p, half), :], partner)
    total_swap.start()
    other_half = spread_piece(links, nh, s, h, beside, later_ref, half, 1 - p)
    kq, vq = r["kq"], r["vq"]
    kvq = kv_ref[pl.ds(pl.multiple_of(h * quarter, 16), quarter), :].astype(F32).T
    kq[...] = kvq[:HEAD_DIM]
    vq[...] = kvq[HEAD_DIM:].astype(BF16)
    xs[...] = scaled(kq[...])
    write_features(kq, xs, f_all.at[0], quarter)
    sback.wait_recv()
    start_gather(other_half)
    for i, k in enumerate(evens):
        kvfirst[i].wait_recv()
        summed = kvl[block(lax.rem(h + k, nh), quarter), :] + kvnear[i]
        if k == nh:
            r["kvsum"][...] = summed
        else:
            kvmid[i] = summed
            to = (s, lax.rem(h + k, nh))
            kvsecond.append(links.copy(kvmid.at[i], kvfar.at[i], to))
            kvsecond[-1].start()
    total_ref[block(p, half), :] = tot[...]
    forward_gather(own_half)
    att_ref[...] = attt[...].T.astype(BF16)
    forward_gather(other_half)
    qg_ref[...] = qgt[...].T.astype(BF16)
    for copy in first + second + smoves + kvfirst + [sback]:
        copy.wait_send()
    total_swap.wait()
    finish_gather(own_half)
    finish_gather(other_half)

    win = r["win"]
    wins = []
    for k in range(nh - 1):
        to = lax.rem(h + k + 1, nh)
        columns = pl.ds(pl.multiple_of(window_at(starts, to, nh), 128), width)
        wins.append(links.copy(total_ref.at[:, columns], win.at[block(h, rows), :], across[k]))
        wins[-1].start()
    own_window = pl.ds(pl.multiple_of(window_at(starts, h, nh), 128), width)
    win[block(h, rows), :] = total_ref[:, own_window]
    later_state = later_ref[...]
    start[...] = later_state.astype(BF16)
    startt[...] = later_state.T.astype(BF16)
    for i, copy in enumerate(kvsecond):
        copy.wait()
        r["kvsum"][...] += kvfar[i]
    gt, part_ref, kv_out = r["gt"], r["part"], r["kv_grad"]
    size = quarter // 2
    gathers = []
    for j in range(2):
        at = slice(j * size, (j + 1) * size)
        gt[HEAD_DIM:, at] = dot(start[...], f_all[0, :, at])
        df[:, at] = dot(startt[...], vq[:, at])
        gt[:HEAD_DIM, at] = feature_grad(xs.at[:, at], df.at[:, at], row.at[:, at], size)
        part_ref[at, :] = r["kvsum"][at, :] + gt[:, at].T
        spot = lambda owner, j=j: block(owner * 2 + j, size)
        gathers.append(gather_copies(links, nh, s, h, beside, part_ref.at[at, :], kv_out, size, spot))
        start_gather(gathers[-1])
    for move in wins:
        move.wait()
    padt[own_window, :] = win[...].T
    kv_out[block(h, quarter), :] = part_ref[...]
    forward_gather(gathers[0])
    canon = r["tall"]
    for a in range(HEAD_DIM):
        at = STARTS[a] + a % 8
        canon[CANON[a] : CANON[a] + HEAD_DIM - a, :] = padt[at : at + HEAD_DIM - a, :]
    slice_width = features // nh
    flip, init_out = r["flip"], r["init_grad"]
    flip[:slice_width, :] = canon[block(h, slice_width), :]
    forward_gather(gathers[1])
    init_out[...] = flip[...].T[:, :slice_width]
    for gather in gathers:
        finish_gather(gather)


def deliver_kernel(count, *refs):
    sems = refs[2 * count]
    copies = [
        pltpu.make_async_copy(refs[i], refs[count + i], sems.at[i]) for i in range(count)
    ]
    for copy in copies:
        copy.start()
    for copy in copies:
        copy.wait()


def deliver(arrays):
    here = pl.BlockSpec(memory_space=pl.ANY)
    return pl.pallas_call(
        functools.partial(deliver_kernel, len(arrays)),
        out_shape=tuple(jax.ShapeDtypeStruct(x.shape, x.dtype) for x in arrays),
        in_specs=[pl.BlockSpec(memory_space=pltpu.VMEM)] * len(arrays),
        out_specs=(here,) * len(arrays),
        scratch_shapes=[pltpu.SemaphoreType.DMA((len(arrays),))],
        compiler_params=pltpu.CompilerParams(vmem_limit_bytes=2 * 1024 * 1024),
    )(*arrays)


def per_device(ns, nh, queries, keys_values, init_state, out_grad):
    tokens, wide = queries.shape
    assert tokens == GROUP and ns % 2 == 0 and nh % 2 == 0 and tokens // nh == CHUNK
    features = init_state.shape[1]
    heads = wide // HEAD_DIM
    rows, quarter, groups = HEAD_DIM // nh, tokens // nh, ns // 2
    even = -(-features // 128) * 128
    starts, width = windows(features, nh)
    slice_width = features // nh
    D, V = pltpu.SemaphoreType.DMA, pltpu.VMEM
    part, piece, state = (rows, PADDED), (rows // 2, PADDED), (HEAD_DIM, PADDED)
    columns, chunk = (wide, tokens), (HEAD_DIM, CHUNK)
    count = 2 + groups - 1 + 2 * (nh - 1)
    count += 2 * (nh - 1) + 3 + groups - 1 + 2 * (nh - 1)
    count += 3 * (nh - 1)
    outs = dict(
        att=((tokens, wide), BF16),
        qg=((tokens, wide), BF16),
        kv_grad=((tokens, 2 * HEAD_DIM), F32),
        init_grad=((HEAD_DIM, slice_width), F32),
    )
    scratch = dict(
        kvt=V((2 * HEAD_DIM, tokens), F32), x=V(chunk, F32), xs=V(chunk, F32), row=V(chunk, F32),
        df=V((PADDED, CHUNK), F32), f=V((tokens // CHUNK * heads, PADDED, CHUNK), BF16),
        qt=V(columns, F32), ogt=V(columns, F32), attt=V(columns, F32), qgt=V(columns, F32),
        dnt=V(columns, BF16), start=V(state, BF16), startt=V((PADDED, HEAD_DIM), BF16),
        keys=V((tokens, HEAD_DIM), BF16), vals=V((tokens, HEAD_DIM), BF16),
        kt=V((HEAD_DIM, tokens), BF16), vt=V((HEAD_DIM, tokens), BF16),
        carry=V(state, F32), later=V(state, F32), sg=V(state, F32),
        kvl=V((tokens, 2 * HEAD_DIM), F32), padt=V((PADDED, HEAD_DIM), F32),
        tall=V((even, HEAD_DIM), F32), wide=V((HEAD_DIM, even), F32),
        u=V(part, F32), pair=V(piece, F32), both=V(piece, F32), mate=V(piece, F32),
        got=V((groups - 1,) + piece, F32),
        near=V((nh // 2,) + part, F32), far=V((nh // 2,) + part, F32),
        mid=V((nh // 2,) + part, F32), own=V(part, F32), spair=V(piece, F32),
        sboth=V(piece, F32), smate=V(piece, F32), tot=V(piece, F32), total=V(part, F32),
        sgot=V((groups - 1,) + piece, F32), kvnear=V((nh // 2, quarter, 2 * HEAD_DIM), F32),
        kvfar=V((nh // 2, quarter, 2 * HEAD_DIM), F32),
        kvmid=V((nh // 2, quarter, 2 * HEAD_DIM), F32),
        initp=V(state, F32),
        kq=V((HEAD_DIM, quarter), F32), vq=V((HEAD_DIM, quarter), BF16),
        kvsum=V((quarter, 2 * HEAD_DIM), F32), gt=V((2 * HEAD_DIM, quarter), F32),
        part=V((quarter, 2 * HEAD_DIM), F32), win=V((HEAD_DIM, width), F32),
        flip=V((-(-slice_width // 128) * 128, HEAD_DIM), F32),
        sends=D((count,)), recvs=D((count,)),
    )
    for c in range(tokens // CHUNK):
        scratch[f"logits{c}"] = V((heads, (c + 1) * CHUNK, CHUNK), F32)
        scratch[f"weights{c}"] = V((heads, (c + 1) * CHUNK, CHUNK), BF16)
    names = ["q", "kv", "init", "og"] + list(outs) + list(scratch)
    vmem = pl.BlockSpec(memory_space=pltpu.VMEM)
    results = pl.pallas_call(
        functools.partial(main_kernel, ns, nh, names, starts, width),
        out_shape=tuple(pltpu.VMEM(*out) for out in outs.values()),
        in_specs=[vmem] * 4,
        out_specs=(vmem,) * len(outs),
        scratch_shapes=list(scratch.values()),
        compiler_params=pltpu.CompilerParams(
            vmem_limit_bytes=58 * 1024 * 1024, collective_id=1, has_side_effects=True
        ),
    )(queries, keys_values, init_state, out_grad)
    return deliver(results)


def solution(mesh):
    ns, nh = mesh.shape["seq"], mesh.shape["head"]
    return jax.shard_map(
        functools.partial(per_device, ns, nh),
        mesh=mesh,
        in_specs=(P("seq", "head"), P("seq", None), P(), P("seq", "head")),
        out_specs=(P("seq", "head"), P("seq", "head"), P("seq", None), P(None, "head")),
        check_vma=False,
    )
```

```python
import functools

import jax
import jax.numpy as jnp
import numpy as np
from jax import lax
from jax.experimental import pallas as pl
from jax.experimental.pallas import tpu as pltpu
from jax.sharding import PartitionSpec as P

HEAD_DIM = 64
GROUP = 1024
EPS = 1e-06
CHUNK = 256
MESH = pl.DeviceIdType.MESH
F32, BF16 = jnp.float32, jnp.bfloat16


def padded_layout(width):
    starts, at = [], 0
    for a in range(width):
        starts.append(at)
        at += width - a // 8 * 8
    return starts, at


STARTS, PADDED = padded_layout(HEAD_DIM)
CANON = [a * HEAD_DIM - a * (a - 1) // 2 for a in range(HEAD_DIM)]


def dot(first, second, contract=((1,), (0,))):
    return lax.dot_general(first, second, (contract, ((), ())), preferred_element_type=F32)


def edge_weights(cols):
    row = lax.broadcasted_iota(jnp.int32, (8, cols), 0)
    return [
        jnp.where(row < m, 0.0, jnp.where(row == m, float(np.sqrt(0.5)), 1.0)).astype(F32)
        for m in range(8)
    ]


def write_features(x_ref, xs_ref, f_ref, cols):
    edges = edge_weights(cols)
    for a in range(0, HEAD_DIM, 2):
        base = a // 8 * 8
        parts = []
        for c in (a, a + 1):
            prod = x_ref[c : c + 1, :] * xs_ref[base:, :]
            parts.append(prod[:8] * edges[c % 8])
            if base + 8 < HEAD_DIM:
                parts.append(prod[8:])
        at = STARTS[a]
        f_ref[at : at + 2 * (HEAD_DIM - base), :] = jnp.concatenate(parts, axis=0).astype(BF16)


def write_window(x_ref, xs_ref, f_ref, cols, first, width):
    edges = edge_weights(cols)
    for a in range(0, HEAD_DIM, 2):
        base = a // 8 * 8
        at, end = STARTS[a], STARTS[a] + 2 * (HEAD_DIM - base)
        lo, hi = max(at, first), min(end, first + width)
        if lo >= hi:
            continue
        parts = []
        for c in (a, a + 1):
            prod = x_ref[c : c + 1, :] * xs_ref[base:, :]
            parts.append(prod[:8] * edges[c % 8])
            if base + 8 < HEAD_DIM:
                parts.append(prod[8:])
        rows = jnp.concatenate(parts, axis=0)[lo - at : hi - at]
        f_ref[lo - first : hi - first, :] = rows.astype(BF16)


def feature_grad(xs_ref, df_ref, row_ref, cols):
    edges = edge_weights(cols)
    tiles = HEAD_DIM // 8
    acc = [jnp.zeros((8, cols), F32) for _ in range(tiles)]
    for a in range(HEAD_DIM):
        first = a // 8
        xa = jnp.broadcast_to(xs_ref[a : a + 1, :], (8, cols))
        total = None
        for t in range(first, tiles):
            at = STARTS[a] + (t - first) * 8
            part = df_ref[at : at + 8, :]
            if t == first:
                part = part * edges[a % 8]
            acc[t] = acc[t] + part * xa
            term = part * xs_ref[t * 8 : t * 8 + 8, :]
            total = term if total is None else total + term
        row_ref[a : a + 1, :] = jnp.sum(total, axis=0, keepdims=True)
    return jnp.concatenate(acc, axis=0) + row_ref[...]


def scaled(x):
    return x * float(np.sqrt(2.0 / HEAD_DIM))


def places(ns, nh):
    s, h = lax.axis_index("seq"), lax.axis_index("head")
    beside = h + 1 - 2 * (h % 2)
    same = [
        (lax.rem(s + k, ns), lax.rem(h + 2 * i, nh))
        for k in range(ns)
        for i in range(nh // 2)
        if (k, i) != (0, 0)
    ]
    other = [(s, lax.rem(beside + 2 * i, nh)) for i in range(nh // 2)]
    return s, h, beside, same + other


def push(src, dst, send, recv, device):
    return pltpu.make_async_remote_copy(
        src_ref=src, dst_ref=dst, send_sem=send, recv_sem=recv,
        device_id=device, device_id_type=MESH,
    )


class Exchange:
    def __init__(self, ns, nh, s, h, beside, heads_in, inbox, outbox, landed, sems):
        self.ns, self.nh, self.s, self.h, self.beside = ns, nh, s, h, beside
        self.groups = HEAD_DIM // 8
        self.step = ns // self.groups
        self.rank, self.pair, self.lane = s // self.step, nh // 2, h // 2
        self.heads_in, self.inbox, self.outbox, self.landed = heads_in, inbox, outbox, landed
        self.in_send, self.in_recv, self.out_send, self.out_recv, self.side_send, self.side_recv = sems

    def own(self, then, otherwise=None):
        if self.step == 1:
            then()
            return
        mine = lax.rem(self.s, self.step) == 0
        pl.when(mine)(then)
        if otherwise is not None:
            pl.when(jnp.logical_not(mine))(otherwise)

    def in_slot(self, k, i):
        at = lax.rem(self.s + k, self.ns)
        return at * self.heads_in + (lax.rem(self.lane + i, self.pair) if self.heads_in > 1 else 0)

    def in_copy(self, piece, i, k):
        to = (lax.rem(self.rank + k, self.groups), lax.rem(self.h + 2 * i, self.nh))
        slot = self.in_slot(0, 0)
        return push(
            piece.at[block(to[0], 8), :], self.inbox.at[slot], self.in_send.at[i * self.groups + k],
            self.in_recv.at[slot], (to[0] * self.step, to[1]),
        )

    def start_in(self, pieces):
        for k in range(1, self.groups + 1):
            for i, piece in enumerate(pieces):
                copy = self.in_copy(piece, i, k % self.groups)
                if i == 0 and k == self.groups:
                    self.own(lambda: self.keep(piece), copy.start)
                else:
                    copy.start()

    def keep(self, piece):
        self.inbox[self.in_slot(0, 0)] = piece[block(self.rank, 8), :]

    def end_in(self, pieces):
        for i, piece in enumerate(pieces):
            for k in range(self.groups):
                copy = self.in_copy(piece, i, k)
                if i == 0 and k == 0:
                    self.own(lambda: None, copy.wait_send)
                else:
                    copy.wait_send()

    def wait_in(self):
        for k in range(self.ns):
            for i in range(self.heads_in):
                if (k, i) != (0, 0):
                    slot = self.in_slot(k, i)
                    box = self.inbox.at[slot]
                    push(box, box, self.in_send.at[0], self.in_recv.at[slot], (self.s, self.beside)).wait_recv()

    def out_copies(self):
        made = []
        for k in range(self.ns):
            n = lax.rem(self.s + k, self.ns)
            for i in range(self.pair):
                if (k, i) != (0, 0):
                    made.append(push(
                        self.outbox.at[n], self.landed.at[self.h, block(self.rank, 8), :],
                        self.out_send.at[k * self.pair + i],
                        self.out_recv.at[self.rank * self.pair + self.lane],
                        (n, lax.rem(self.h + 2 * i, self.nh)),
                    ))
        return made

    def start_out(self):
        for copy in self.out_copies():
            copy.start()
        self.landed[self.h, block(self.rank, 8), :] = self.outbox[self.s]

    def end_out(self):
        for copy in self.out_copies():
            copy.wait_send()

    def wait_out(self, i):
        window = lax.rem(self.h + 2 * i, self.nh)
        for k in range(self.groups):
            j, lane = lax.rem(self.rank + k, self.groups), window // 2
            box = self.landed.at[window, block(j, 8), :]
            copy = push(
                box, box, self.out_send.at[0], self.out_recv.at[j * self.pair + lane], (self.s, self.beside)
            )
            if (k, i) == (0, 0):
                self.own(lambda: None, copy.wait_recv)
            else:
                copy.wait_recv()

    def side_copy(self, i, head):
        window = lax.rem(head + 2 * i, self.nh)
        box = self.landed.at[window]
        return push(
            box, box, self.side_send.at[window // 2], self.side_recv.at[window // 2], (self.s, self.beside)
        )


def block(index, size):
    return pl.ds(pl.multiple_of(index * size, 8), size)


class Links:
    def __init__(self, sends, recvs):
        self.sends, self.recvs, self.used = sends, recvs, 0

    def copy(self, src, dst, device):
        k = self.used
        self.used += 1
        return pltpu.make_async_remote_copy(
            src_ref=src, dst_ref=dst, send_sem=self.sends.at[k], recv_sem=self.recvs.at[k],
            device_id=device, device_id_type=MESH,
        )


def gather_copies(links, nh, s, h, beside, src, out, size, spot):
    far = []
    for k in range(2, nh, 2):
        to = lax.rem(h + k, nh)
        first = links.copy(src, out.at[spot(h)], (s, to))
        came = out.at[spot(lax.rem(h + nh - k, nh))]
        far.append((first, links.copy(came, came, (s, beside))))
    near = links.copy(src, out.at[spot(h)], (s, beside))
    return far, near


def start_gather(gather):
    far, near = gather
    for first, _ in far:
        first.start()
    near.start()


def forward_gather(gather):
    for first, second in gather[0]:
        first.wait_recv()
        second.start()


def finish_gather(gather):
    far, near = gather
    for first, second in far:
        first.wait_send()
        second.wait()
    near.wait()


def padded_column(c):
    a = max(a for a in range(HEAD_DIM) if CANON[a] <= c)
    return STARTS[a] + a % 8 + c - CANON[a]


def windows(features, nh):
    wide = features // nh
    ends = [(padded_column(k * wide), padded_column(k * wide + wide - 1)) for k in range(nh)]
    starts = [lo // 16 * 16 for lo, _ in ends]
    width = max(-(-(hi + 1 - lo) // 128) * 128 for lo, (_, hi) in zip(starts, ends))
    starts = [min(lo, PADDED - width) for lo in starts]
    assert starts[0] == 0 and all(b - a <= width for a, b in zip(starts, starts[1:]))
    return starts, width


def joined(landed, starts):
    ends = starts[1:] + [PADDED]
    return jnp.concatenate(
        [landed[k].T[: ends[k] - starts[k]] for k in range(len(starts))], axis=0
    )


def window_at(starts, owner, nh):
    at = starts[0]
    for k in range(1, nh):
        at = at + (starts[k] - starts[k - 1]) * ((owner + nh - k) // nh)
    return at


def masked(full, causal):
    n = full.shape[0]
    last = jnp.where(causal, full[n - CHUNK :], 0.0)
    if n == CHUNK:
        return last.astype(BF16)
    return jnp.concatenate([full[: n - CHUNK], last], axis=0).astype(BF16)


def main_kernel(ns, nh, names, starts, width, *refs):
    r = dict(zip(names, refs))
    q_ref, kv_ref, init_ref, og_ref = r["q"], r["kv"], r["init"], r["og"]
    kvt, xs, x, row, df, f_all = r["kvt"], r["xs"], r["x"], r["row"], r["df"], r["f"]
    qt, ogt, attt, qgt, dnt = r["qt"], r["ogt"], r["attt"], r["qgt"], r["dnt"]
    start, startt, keys, vals, kt, vt = (
        r["start"], r["startt"], r["keys"], r["vals"], r["kt"], r["vt"]
    )
    sg, kvl = r["sg"], r["kvl"]
    padt, tall = r["padt"], r["tall"]
    tokens = q_ref.shape[0]
    heads = q_ref.shape[1] // HEAD_DIM
    chunks = tokens // CHUNK
    features = init_ref.shape[1]
    quarter = tokens // nh
    s, h, beside, peers = places(ns, nh)
    links = Links(r["sends"], r["recvs"])
    sems = lambda name: [r[name + x] for x in ("is", "ir", "os", "or", "ss", "sr")]
    early = Exchange(ns, nh, s, h, beside, 1, r["inbox"], r["outbox"], r["carry"], sems("a"))
    late = Exchange(ns, nh, s, h, beside, nh // 2, r["sinbox"], r["soutbox"], r["later"], sems("c"))
    barrier = pltpu.get_barrier_semaphore()
    for device in peers:
        pl.semaphore_signal(barrier, inc=1, device_id=device, device_id_type=MESH)

    kvt[...] = kv_ref[...].astype(F32).T
    vt[...] = kvt[HEAD_DIM:, :].astype(BF16)
    u_ref = r["u"]
    for c in range(chunks):
        at = slice(c * CHUNK, (c + 1) * CHUNK)
        xs[...] = scaled(kvt[:HEAD_DIM, at])
        for k in range(nh):
            @pl.when(h == k)
            def _(c=c, at=at, k=k):
                write_window(kvt.at[:HEAD_DIM, at], xs, f_all.at[c], CHUNK, starts[k], width)
    u_ref[...] = sum(
        dot(vt[:, c * CHUNK : (c + 1) * CHUNK], f_all[c, :width, :], ((1,), (1,)))
        for c in range(chunks)
    )
    pl.semaphore_wait(barrier, len(peers))
    early.start_in([u_ref])

    qt[...] = q_ref[...].astype(F32).T
    kt[...] = kvt[:HEAD_DIM, :].astype(BF16)
    keys[...] = kv_ref[:, :HEAD_DIM]
    vals[...] = kv_ref[:, HEAD_DIM:]
    causal = lax.broadcasted_iota(jnp.int32, (CHUNK, CHUNK), 0) <= lax.broadcasted_iota(
        jnp.int32, (CHUNK, CHUNK), 1
    )

    def inner(c):
        n = (c + 1) * CHUNK
        at = slice(c * CHUNK, n)

        def one_head(k, _):
            here = pl.ds(pl.multiple_of(k * HEAD_DIM, HEAD_DIM), HEAD_DIM)
            query = qt[here, at]
            x[...] = query
            xs[...] = scaled(query)
            write_features(x, xs, f_all.at[c * heads + k], CHUNK)
            logits = dot(keys[:n], query.astype(BF16))
            weights = masked(logits * logits * (1.0 / HEAD_DIM), causal)
            r[f"logits{c}"][k] = logits
            r[f"weights{c}"][k] = weights
            attt[here, at] = dot(vt[:, :n], weights)
            return 0

        lax.fori_loop(0, heads, one_head, 0)

    def upward(c):
        n = (c + 1) * CHUNK
        at = slice(c * CHUNK, n)

        def one_head(k, _):
            here = pl.ds(pl.multiple_of(k * HEAD_DIM, HEAD_DIM), HEAD_DIM)
            query = qt[here, at]
            xs[...] = scaled(query)
            dn = dnt[here, at]
            df[...] = dot(startt[...], dn)
            dw = dot(vals[:n], dn)
            dl = masked(dw * r[f"logits{c}"][k] * (2.0 / HEAD_DIM), causal)
            qgt[here, at] = dot(kt[:, :n], dl) + feature_grad(xs, df, row, CHUNK)
            kvl[:n, :HEAD_DIM] += dot(dl, query.astype(BF16), ((1,), (1,)))
            kvl[:n, HEAD_DIM:] += dot(r[f"weights{c}"][k], dn, ((1,), (1,)))
            return 0

        lax.fori_loop(0, heads, one_head, 0, unroll=True)

    wide = r["wide"]
    whole_lanes = features // 128 * 128
    padt[...] = jnp.zeros_like(padt)
    wide[:, whole_lanes:] = jnp.zeros_like(wide[:, whole_lanes:])
    wide[:, :features] = init_ref[...]
    tall[...] = wide[...].T
    for a in range(HEAD_DIM):
        at = STARTS[a] + a % 8
        padt[at : at + HEAD_DIM - a, :] = tall[CANON[a] : CANON[a] + HEAD_DIM - a, :]
    ogt[...] = og_ref[...].astype(F32).T
    order = list(range(chunks))
    for c in order[:1:-1]:
        inner(c)

    def prefixes():
        early.wait_in()
        total = jnp.zeros_like(r["inbox"][0])
        for m in range(ns):
            r["outbox"][m] = total
            total = total + r["inbox"][m]
        early.start_out()

    early.own(prefixes)
    for c in order[1::-1]:
        inner(c)
    pairs = range(nh // 2)
    for i in pairs:
        early.wait_out(i)
        early.side_copy(i, h).start()
    early.end_in([u_ref])
    early.own(early.end_out)
    for i in pairs:
        early.side_copy(i, beside).wait_recv()
        early.side_copy(i, h).wait_send()
    first_state = padt[...] + joined(r["carry"], starts)
    startt[...] = first_state.astype(BF16)
    start[...] = first_state.T.astype(BF16)

    def normalize(c, _):
        at = pl.ds(pl.multiple_of(c * CHUNK, CHUNK), CHUNK)
        for k in range(heads):
            here = slice(k * HEAD_DIM, (k + 1) * HEAD_DIM)
            numer = attt[here, at] + dot(start[...], f_all[c * heads + k])
            scale = lax.rsqrt(jnp.mean(numer * numer, axis=0, keepdims=True) + EPS)
            normed = numer * scale
            up = ogt[here, at]
            attt[here, at] = normed
            dn = (scale * (up - normed * jnp.mean(up * normed, axis=0, keepdims=True))).astype(BF16)
            dnt[here, at] = dn
        return 0

    lax.fori_loop(0, chunks, normalize, 0, unroll=True)

    def state_columns(t, _):
        cols = pl.ds(pl.multiple_of(t * CHUNK, CHUNK), CHUNK)
        sg[:, cols] = sum(
            dot(
                dnt[k * HEAD_DIM : (k + 1) * HEAD_DIM, c * CHUNK : (c + 1) * CHUNK],
                f_all[c * heads + k, cols, :],
                ((1,), (1,)),
            )
            for c in range(chunks)
            for k in range(heads)
        )
        return 0

    lax.fori_loop(0, PADDED // CHUNK, state_columns, 0, unroll=3)

    near, sgw = r["near"], r["sgw"]
    for k in range(nh):
        lo = starts[k] // 128 * 128
        off = starts[k] - lo
        if off:
            span = width + 128
            sgw[k] = pltpu.roll(sg[:, lo : lo + span], span - off, 1)[:, :width]
        else:
            sgw[k] = sg[:, lo : lo + width]
    def swap(i, head):
        window = lax.rem(head + 2 * i, nh)
        return push(
            sgw.at[window], near.at[window // 2], r["ns"].at[window // 2],
            r["nr"].at[window // 2], (s, beside),
        )

    for i in pairs:
        swap(i, beside).start()
    kvl[...] = jnp.zeros_like(kvl)
    upward(0)
    mids = [r["mid"].at[i] for i in pairs]
    for i in pairs:
        window = lax.rem(h + 2 * i, nh)
        swap(i, h).wait_recv()
        r["mid"][i] = sgw[window] + near[window // 2]
    late.start_in(mids)
    for c in order[:1:-1]:
        upward(c)
    tot, win = r["tot"], r["win"]

    def total_copies():
        return [
            push(
                tot, win.at[block(late.rank, 8), :], r["ts"].at[k], r["tr"].at[late.rank],
                (lax.rem(s + k, ns), h),
            )
            for k in range(1, ns)
        ]

    def suffixes():
        late.wait_in()
        total = jnp.zeros_like(r["sinbox"][0])
        for m in reversed(range(ns)):
            r["soutbox"][m] = total
            for i in pairs:
                total = total + r["sinbox"][m * (nh // 2) + i]
        tot[...] = total
        late.start_out()
        for copy in total_copies():
            copy.start()
        win[block(late.rank, 8), :] = total

    late.own(suffixes)
    upward(1)
    kvnear, kvfar, kvmid = r["kvnear"], r["kvfar"], r["kvmid"]
    evens = range(2, nh + 1, 2)
    kvfirst, kvsecond = [], []
    for i, k in enumerate(evens):
        src = kvl.at[block(lax.rem(beside + k, nh), quarter), :]
        kvfirst.append(links.copy(src, kvnear.at[i], (s, beside)))
        kvfirst[-1].start()
    kq, vq = r["kq"], r["vq"]
    kvq = kv_ref[pl.ds(pl.multiple_of(h * quarter, 16), quarter), :].astype(F32).T
    kq[...] = kvq[:HEAD_DIM]
    vq[...] = kvq[HEAD_DIM:].astype(BF16)
    xs[...] = scaled(kq[...])
    write_features(kq, xs, f_all.at[0], quarter)
    for i, k in enumerate(evens):
        kvfirst[i].wait_recv()
        summed = kvl[block(lax.rem(h + k, nh), quarter), :] + kvnear[i]
        if k == nh:
            r["kvsum"][...] = summed
        else:
            kvmid[i] = summed
            to = (s, lax.rem(h + k, nh))
            kvsecond.append(links.copy(kvmid.at[i], kvfar.at[i], to))
            kvsecond[-1].start()
    att_ref, qg_ref = r["att"], r["qg"]
    att_ref[...] = attt[...].T.astype(BF16)
    qg_ref[...] = qgt[...].T.astype(BF16)
    for copy in kvfirst + [swap(i, beside) for i in pairs]:
        copy.wait_send()
    for i in pairs:
        late.wait_out(i)
        late.side_copy(i, h).start()
    late.end_in(mids)
    late.own(late.end_out)
    for i, copy in enumerate(kvsecond):
        copy.wait()
        r["kvsum"][...] += kvfar[i]
    for i in pairs:
        late.side_copy(i, beside).wait_recv()
        late.side_copy(i, h).wait_send()
    later_state = joined(r["later"], starts)
    startt[...] = later_state.astype(BF16)
    start[...] = later_state.T.astype(BF16)
    gt, part_ref, kv_out = r["gt"], r["part"], r["kv_grad"]
    size = quarter // 2
    gathers = []
    for j in range(2):
        at = slice(j * size, (j + 1) * size)
        gt[HEAD_DIM:, at] = dot(start[...], f_all[0, :, at])
        df[:, at] = dot(startt[...], vq[:, at])
        gt[:HEAD_DIM, at] = feature_grad(xs.at[:, at], df.at[:, at], row.at[:, at], size)
        part_ref[at, :] = r["kvsum"][at, :] + gt[:, at].T
        spot = lambda owner, j=j: block(owner * 2 + j, size)
        gathers.append(gather_copies(links, nh, s, h, beside, part_ref.at[at, :], kv_out, size, spot))
        start_gather(gathers[-1])
    for k in range(late.groups):
        j = lax.rem(late.rank + k, late.groups)
        box = win.at[block(j, 8), :]
        copy = push(box, box, r["ts"].at[0], r["tr"].at[j], (s, beside))
        if k == 0:
            late.own(lambda: None, copy.wait_recv)
        else:
            copy.wait_recv()

    def end_totals():
        for copy in total_copies():
            copy.wait_send()

    late.own(end_totals)
    own_window = pl.ds(pl.multiple_of(window_at(starts, h, nh), 16), width)
    padt[own_window, :] = win[...].T
    kv_out[block(h, quarter), :] = part_ref[...]
    forward_gather(gathers[0])
    canon = r["tall"]
    for a in range(HEAD_DIM):
        at = STARTS[a] + a % 8
        canon[CANON[a] : CANON[a] + HEAD_DIM - a, :] = padt[at : at + HEAD_DIM - a, :]
    slice_width = features // nh
    flip, init_out = r["flip"], r["init_grad"]
    flip[:slice_width, :] = canon[block(h, slice_width), :]
    forward_gather(gathers[1])
    init_out[...] = flip[...].T[:, :slice_width]
    for gather in gathers:
        finish_gather(gather)


def deliver_kernel(count, *refs):
    sems = refs[2 * count]
    copies = [
        pltpu.make_async_copy(refs[i], refs[count + i], sems.at[i]) for i in range(count)
    ]
    for copy in copies:
        copy.start()
    for copy in copies:
        copy.wait()


def deliver(arrays):
    here = pl.BlockSpec(memory_space=pl.ANY)
    return pl.pallas_call(
        functools.partial(deliver_kernel, len(arrays)),
        out_shape=tuple(jax.ShapeDtypeStruct(x.shape, x.dtype) for x in arrays),
        in_specs=[pl.BlockSpec(memory_space=pltpu.VMEM)] * len(arrays),
        out_specs=(here,) * len(arrays),
        scratch_shapes=[pltpu.SemaphoreType.DMA((len(arrays),))],
        compiler_params=pltpu.CompilerParams(vmem_limit_bytes=2 * 1024 * 1024),
    )(*arrays)


def per_device(ns, nh, queries, keys_values, init_state, out_grad):
    tokens, wide = queries.shape
    assert tokens == GROUP and ns % 8 == 0 and nh % 2 == 0 and tokens // nh == CHUNK
    features = init_state.shape[1]
    heads = wide // HEAD_DIM
    quarter, pair, groups = tokens // nh, nh // 2, HEAD_DIM // 8
    even = -(-features // 128) * 128
    starts, width = windows(features, nh)
    slice_width = features // nh
    D, V = pltpu.SemaphoreType.DMA, pltpu.VMEM
    state, piece, window = (HEAD_DIM, PADDED), (8, width), (HEAD_DIM, width)
    columns, chunk = (wide, tokens), (HEAD_DIM, CHUNK)
    count = 2 * (nh - 1) + 3 * (nh - 1)
    outs = dict(
        att=((tokens, wide), BF16),
        qg=((tokens, wide), BF16),
        kv_grad=((tokens, 2 * HEAD_DIM), F32),
        init_grad=((HEAD_DIM, slice_width), F32),
    )
    scratch = dict(
        kvt=V((2 * HEAD_DIM, tokens), F32), x=V(chunk, F32), xs=V(chunk, F32), row=V(chunk, F32),
        df=V((PADDED, CHUNK), F32), f=V((tokens // CHUNK * heads, PADDED, CHUNK), BF16),
        qt=V(columns, F32), ogt=V(columns, F32), attt=V(columns, F32), qgt=V(columns, F32),
        dnt=V(columns, BF16), start=V(state, BF16), startt=V((PADDED, HEAD_DIM), BF16),
        keys=V((tokens, HEAD_DIM), BF16), vals=V((tokens, HEAD_DIM), BF16),
        kt=V((HEAD_DIM, tokens), BF16), vt=V((HEAD_DIM, tokens), BF16),
        sg=V(state, F32), carry=V((nh,) + window, F32), later=V((nh,) + window, F32),
        kvl=V((tokens, 2 * HEAD_DIM), F32), padt=V((PADDED, HEAD_DIM), F32),
        tall=V((even, HEAD_DIM), F32), wide=V((HEAD_DIM, even), F32),
        u=V(window, F32), inbox=V((ns,) + piece, F32), outbox=V((ns,) + piece, F32),
        sinbox=V((ns * pair,) + piece, F32), soutbox=V((ns,) + piece, F32), tot=V(piece, F32),
        near=V((pair,) + window, F32), mid=V((pair,) + window, F32), sgw=V((nh,) + window, F32),
        kvnear=V((nh // 2, quarter, 2 * HEAD_DIM), F32),
        kvfar=V((nh // 2, quarter, 2 * HEAD_DIM), F32),
        kvmid=V((nh // 2, quarter, 2 * HEAD_DIM), F32),
        kq=V((HEAD_DIM, quarter), F32), vq=V((HEAD_DIM, quarter), BF16),
        kvsum=V((quarter, 2 * HEAD_DIM), F32), gt=V((2 * HEAD_DIM, quarter), F32),
        part=V((quarter, 2 * HEAD_DIM), F32), win=V((HEAD_DIM, width), F32),
        flip=V((-(-slice_width // 128) * 128, HEAD_DIM), F32),
        sends=D((count,)), recvs=D((count,)), ns=D((pair,)), nr=D((pair,)), ts=D((ns,)), tr=D((groups,)),
        ais=D((groups,)), air=D((ns,)), cis=D((groups * pair,)), cir=D((ns * pair,)),
    )
    for name in ("a", "c"):
        scratch[name + "os"], scratch[name + "or"] = D((ns * pair,)), D((groups * pair,))
        scratch[name + "ss"], scratch[name + "sr"] = D((pair,)), D((pair,))
    for c in range(tokens // CHUNK):
        scratch[f"logits{c}"] = V((heads, (c + 1) * CHUNK, CHUNK), F32)
        scratch[f"weights{c}"] = V((heads, (c + 1) * CHUNK, CHUNK), BF16)
    names = ["q", "kv", "init", "og"] + list(outs) + list(scratch)
    vmem = pl.BlockSpec(memory_space=pltpu.VMEM)
    results = pl.pallas_call(
        functools.partial(main_kernel, ns, nh, names, starts, width),
        out_shape=tuple(pltpu.VMEM(*out) for out in outs.values()),
        in_specs=[vmem] * 4,
        out_specs=(vmem,) * len(outs),
        scratch_shapes=list(scratch.values()),
        compiler_params=pltpu.CompilerParams(
            vmem_limit_bytes=58 * 1024 * 1024, collective_id=1, has_side_effects=True
        ),
    )(queries, keys_values, init_state, out_grad)
    return deliver(results)


def solution(mesh):
    ns, nh = mesh.shape["seq"], mesh.shape["head"]
    return jax.shard_map(
        functools.partial(per_device, ns, nh),
        mesh=mesh,
        in_specs=(P("seq", "head"), P("seq", None), P(), P("seq", "head")),
        out_specs=(P("seq", "head"), P("seq", "head"), P("seq", None), P(None, "head")),
        check_vma=False,
    )
```

```python
import functools

import jax
import jax.numpy as jnp
import numpy as np
from jax import lax
from jax.experimental import pallas as pl
from jax.experimental.pallas import tpu as pltpu
from jax.sharding import PartitionSpec as P

HEAD_DIM = 64
GROUP = 1024
EPS = 1e-06
CHUNK = 256
MESH = pl.DeviceIdType.MESH
F32, BF16 = jnp.float32, jnp.bfloat16


def padded_layout(width):
    starts, at = [], 0
    for a in range(width):
        starts.append(at)
        at += width - a // 8 * 8
    return starts, at


STARTS, PADDED = padded_layout(HEAD_DIM)
CANON = [a * HEAD_DIM - a * (a - 1) // 2 for a in range(HEAD_DIM)]


def dot(first, second, contract=((1,), (0,))):
    return lax.dot_general(first, second, (contract, ((), ())), preferred_element_type=F32)


def edge_weights(cols):
    row = lax.broadcasted_iota(jnp.int32, (8, cols), 0)
    return [
        jnp.where(row < m, 0.0, jnp.where(row == m, float(np.sqrt(0.5)), 1.0)).astype(F32)
        for m in range(8)
    ]


def write_features(x_ref, xs_ref, f_ref, cols):
    edges = edge_weights(cols)
    for a in range(0, HEAD_DIM, 2):
        base = a // 8 * 8
        parts = []
        for c in (a, a + 1):
            prod = x_ref[c : c + 1, :] * xs_ref[base:, :]
            parts.append(prod[:8] * edges[c % 8])
            if base + 8 < HEAD_DIM:
                parts.append(prod[8:])
        at = STARTS[a]
        f_ref[at : at + 2 * (HEAD_DIM - base), :] = jnp.concatenate(parts, axis=0).astype(BF16)


def write_window(x_ref, xs_ref, f_ref, cols, first, width):
    edges = edge_weights(cols)
    for a in range(0, HEAD_DIM, 2):
        base = a // 8 * 8
        at, end = STARTS[a], STARTS[a] + 2 * (HEAD_DIM - base)
        lo, hi = max(at, first), min(end, first + width)
        if lo >= hi:
            continue
        parts = []
        for c in (a, a + 1):
            prod = x_ref[c : c + 1, :] * xs_ref[base:, :]
            parts.append(prod[:8] * edges[c % 8])
            if base + 8 < HEAD_DIM:
                parts.append(prod[8:])
        rows = jnp.concatenate(parts, axis=0)[lo - at : hi - at]
        f_ref[lo - first : hi - first, :] = rows.astype(BF16)


def feature_grad(xs_ref, df_ref, row_ref, cols, ranges=((0, PADDED),)):
    edges = edge_weights(cols)
    tiles = HEAD_DIM // 8
    acc = [jnp.zeros((8, cols), F32) for _ in range(tiles)]
    for a in range(HEAD_DIM):
        first = a // 8
        xa = jnp.broadcast_to(xs_ref[a : a + 1, :], (8, cols))
        total = None
        for t in range(first, tiles):
            at = STARTS[a] + (t - first) * 8
            if not any(lo <= at < hi for lo, hi in ranges):
                continue
            part = df_ref[at : at + 8, :]
            if t == first:
                part = part * edges[a % 8]
            acc[t] = acc[t] + part * xa
            term = part * xs_ref[t * 8 : t * 8 + 8, :]
            total = term if total is None else total + term
        if total is None:
            total = jnp.zeros((8, cols), F32)
        row_ref[a : a + 1, :] = jnp.sum(total, axis=0, keepdims=True)
    return jnp.concatenate(acc, axis=0) + row_ref[...]


def scaled(x):
    return x * float(np.sqrt(2.0 / HEAD_DIM))


def places(ns, nh):
    s, h = lax.axis_index("seq"), lax.axis_index("head")
    beside = h + 1 - 2 * (h % 2)
    same = [
        (lax.rem(s + k, ns), lax.rem(h + 2 * i, nh))
        for k in range(ns)
        for i in range(nh // 2)
        if (k, i) != (0, 0)
    ]
    other = [(s, lax.rem(beside + 2 * i, nh)) for i in range(nh // 2)]
    return s, h, beside, same + other


def push(src, dst, send, recv, device):
    return pltpu.make_async_remote_copy(
        src_ref=src, dst_ref=dst, send_sem=send, recv_sem=recv,
        device_id=device, device_id_type=MESH,
    )


class Exchange:
    def __init__(self, ns, nh, s, h, beside, heads_in, inbox, outbox, landed, sems):
        self.ns, self.nh, self.s, self.h, self.beside = ns, nh, s, h, beside
        self.groups = HEAD_DIM // 8
        self.step = ns // self.groups
        self.rank, self.pair, self.lane = s // self.step, nh // 2, h // 2
        self.heads_in, self.inbox, self.outbox, self.landed = heads_in, inbox, outbox, landed
        self.in_send, self.in_recv, self.out_send, self.out_recv = sems[:4]
        self.side = sems[4:]

    def own(self, then, otherwise=None):
        if self.step == 1:
            then()
            return
        mine = lax.rem(self.s, self.step) == 0
        pl.when(mine)(then)
        if otherwise is not None:
            pl.when(jnp.logical_not(mine))(otherwise)

    def in_slot(self, k, i):
        at = lax.rem(self.s + k, self.ns)
        return at * self.heads_in + (lax.rem(self.lane + i, self.pair) if self.heads_in > 1 else 0)

    def in_copy(self, piece, i, k):
        to = (lax.rem(self.rank + k, self.groups), lax.rem(self.h + 2 * i, self.nh))
        slot = self.in_slot(0, 0)
        return push(
            piece.at[block(to[0], 8), :], self.inbox.at[slot], self.in_send.at[i * self.groups + k],
            self.in_recv.at[slot], (to[0] * self.step, to[1]),
        )

    def start_in(self, piece, i=0):
        for k in range(1, self.groups + 1):
            copy = self.in_copy(piece, i, k % self.groups)
            if i == 0 and k == self.groups:
                self.own(lambda: self.keep(piece), copy.start)
            else:
                copy.start()

    def keep(self, piece):
        self.inbox[self.in_slot(0, 0)] = piece[block(self.rank, 8), :]

    def end_in(self, pieces):
        for i, piece in enumerate(pieces):
            for k in range(self.groups):
                copy = self.in_copy(piece, i, k)
                if i == 0 and k == 0:
                    self.own(lambda: None, copy.wait_send)
                else:
                    copy.wait_send()

    def wait_in(self):
        for k in range(self.ns):
            for i in range(self.heads_in):
                if (k, i) != (0, 0):
                    slot = self.in_slot(k, i)
                    box = self.inbox.at[slot]
                    push(box, box, self.in_send.at[0], self.in_recv.at[slot], (self.s, self.beside)).wait_recv()

    def out_copies(self):
        made = []
        for i in range(self.pair):
            for k in range(self.ns):
                n = lax.rem(self.s + k, self.ns)
                if (k, i) != (0, 0):
                    made.append(push(
                        self.outbox.at[n], self.landed.at[self.h, block(self.rank, 8), :],
                        self.out_send.at[k * self.pair + i],
                        self.out_recv.at[self.rank * self.pair + self.lane],
                        (n, lax.rem(self.h + 2 * i, self.nh)),
                    ))
        return made

    def start_out(self):
        for copy in self.out_copies():
            copy.start()
        self.landed[self.h, block(self.rank, 8), :] = self.outbox[self.s]

    def end_out(self):
        for copy in self.out_copies():
            copy.wait_send()

    def wait_out(self, i):
        window = lax.rem(self.h + 2 * i, self.nh)
        for k in range(self.groups):
            j, lane = lax.rem(self.rank + k, self.groups), window // 2
            box = self.landed.at[window, block(j, 8), :]
            copy = push(
                box, box, self.out_send.at[0], self.out_recv.at[j * self.pair + lane], (self.s, self.beside)
            )
            if (k, i) == (0, 0):
                self.own(lambda: None, copy.wait_recv)
            else:
                copy.wait_recv()

    def side_copy(self, i, head):
        window = lax.rem(head + 2 * i, self.nh)
        box = self.landed.at[window]
        return push(
            box, box, self.side[0].at[window // 2], self.side[1].at[window // 2], (self.s, self.beside)
        )


def block(index, size):
    return pl.ds(pl.multiple_of(index * size, 8), size)


class Links:
    def __init__(self, sends, recvs):
        self.sends, self.recvs, self.used = sends, recvs, 0

    def copy(self, src, dst, device):
        k = self.used
        self.used += 1
        return pltpu.make_async_remote_copy(
            src_ref=src, dst_ref=dst, send_sem=self.sends.at[k], recv_sem=self.recvs.at[k],
            device_id=device, device_id_type=MESH,
        )


def padded_column(c):
    a = max(a for a in range(HEAD_DIM) if CANON[a] <= c)
    return STARTS[a] + a % 8 + c - CANON[a]


def windows(features, nh):
    wide = features // nh
    ends = [(padded_column(k * wide), padded_column(k * wide + wide - 1)) for k in range(nh)]
    starts = [lo // 16 * 16 for lo, _ in ends]
    width = max(-(-(hi + 1 - lo) // 128) * 128 for lo, (_, hi) in zip(starts, ends))
    starts = [min(lo, PADDED - width) for lo in starts]
    assert starts[0] == 0 and all(b - a <= width for a, b in zip(starts, starts[1:]))
    return starts, width


def joined(landed, starts):
    ends = starts[1:] + [PADDED]
    return jnp.concatenate(
        [landed[k].T[: ends[k] - starts[k]] for k in range(len(starts))], axis=0
    )


def window_at(starts, owner, nh):
    at = starts[0]
    for k in range(1, nh):
        at = at + (starts[k] - starts[k - 1]) * ((owner + nh - k) // nh)
    return at


def masked(full, causal):
    n = full.shape[0]
    last = jnp.where(causal, full[n - CHUNK :], 0.0)
    if n == CHUNK:
        return last.astype(BF16)
    return jnp.concatenate([full[: n - CHUNK], last], axis=0).astype(BF16)


def main_kernel(ns, nh, names, starts, width, *refs):
    r = dict(zip(names, refs))
    q_ref, kv_ref, init_ref, og_ref = r["q"], r["kv"], r["init"], r["og"]
    kvt, xs, x, row, df, f_all = r["kvt"], r["xs"], r["x"], r["row"], r["df"], r["f"]
    qt, ogt, attt, qgt, dnt = r["qt"], r["ogt"], r["attt"], r["qgt"], r["dnt"]
    startt, keys, vals, kt, vt = r["startt"], r["keys"], r["vals"], r["kt"], r["vt"]
    kvl = r["kvl"]
    padt, tall = r["padt"], r["tall"]
    tokens = q_ref.shape[0]
    heads = q_ref.shape[1] // HEAD_DIM
    chunks = tokens // CHUNK
    features = init_ref.shape[1]
    s, h, beside, peers = places(ns, nh)
    links = Links(r["sends"], r["recvs"])
    sems = lambda name: [r[name + x] for x in ("is", "ir", "os", "or", "ss", "sr") if name + x in r]
    early = Exchange(ns, nh, s, h, beside, 1, r["inbox"], r["outbox"], r["carry"], sems("a"))
    late = Exchange(ns, nh, s, h, beside, nh // 2, r["sinbox"], r["soutbox"], r["later"], sems("c"))
    barrier = pltpu.get_barrier_semaphore()
    for device in peers:
        pl.semaphore_signal(barrier, inc=1, device_id=device, device_id_type=MESH)

    kvt[...] = kv_ref[...].astype(F32).T
    vt[...] = kvt[HEAD_DIM:, :].astype(BF16)
    u_ref = r["u"]
    for c in range(chunks):
        at = slice(c * CHUNK, (c + 1) * CHUNK)
        xs[...] = scaled(kvt[:HEAD_DIM, at])
        for k in range(nh):
            @pl.when(h == k)
            def _(c=c, at=at, k=k):
                write_window(kvt.at[:HEAD_DIM, at], xs, f_all.at[c], CHUNK, starts[k], width)
    u_ref[...] = sum(
        dot(vt[:, c * CHUNK : (c + 1) * CHUNK], f_all[c, :width, :], ((1,), (1,)))
        for c in range(chunks)
    )
    pl.semaphore_wait(barrier, len(peers))
    early.start_in(u_ref)

    qt[...] = q_ref[...].astype(F32).T
    kt[...] = kvt[:HEAD_DIM, :].astype(BF16)
    keys[...] = kv_ref[:, :HEAD_DIM]
    vals[...] = kv_ref[:, HEAD_DIM:]
    causal = lax.broadcasted_iota(jnp.int32, (CHUNK, CHUNK), 0) <= lax.broadcasted_iota(
        jnp.int32, (CHUNK, CHUNK), 1
    )

    def inner(c):
        n = (c + 1) * CHUNK
        at = slice(c * CHUNK, n)

        def one_head(k, _):
            here = pl.ds(pl.multiple_of(k * HEAD_DIM, HEAD_DIM), HEAD_DIM)
            query = qt[here, at]
            x[...] = query
            xs[...] = scaled(query)
            write_features(x, xs, f_all.at[c * heads + k], CHUNK)
            logits = dot(keys[:n], query.astype(BF16))
            weights = masked(logits * logits * (1.0 / HEAD_DIM), causal)
            r[f"logits{c}"][k] = logits
            r[f"weights{c}"][k] = weights
            attt[here, at] = dot(vt[:, :n], weights)
            return 0

        lax.fori_loop(0, heads, one_head, 0)

    def upward(c):
        n = (c + 1) * CHUNK
        at = slice(c * CHUNK, n)

        def one_head(k, _):
            here = pl.ds(pl.multiple_of(k * HEAD_DIM, HEAD_DIM), HEAD_DIM)
            query = qt[here, at]
            xs[...] = scaled(query)
            dn = dnt[here, at]
            df[...] = dot(startt[...], dn)
            dw = dot(vals[:n], dn)
            dl = masked(dw * r[f"logits{c}"][k] * (2.0 / HEAD_DIM), causal)
            qgt[here, at] = dot(kt[:, :n], dl) + feature_grad(xs, df, row, CHUNK)
            kvl[:n, :HEAD_DIM] += dot(dl, query.astype(BF16), ((1,), (1,)))
            kvl[:n, HEAD_DIM:] += dot(r[f"weights{c}"][k], dn, ((1,), (1,)))
            return 0

        lax.fori_loop(0, heads, one_head, 0, unroll=True)

    wide = r["wide"]
    whole_lanes = features // 128 * 128
    padt[...] = jnp.zeros_like(padt)
    wide[:, whole_lanes:] = jnp.zeros_like(wide[:, whole_lanes:])
    wide[:, :features] = init_ref[...]
    tall[...] = wide[...].T
    for a in range(HEAD_DIM):
        at = STARTS[a] + a % 8
        padt[at : at + HEAD_DIM - a, :] = tall[CANON[a] : CANON[a] + HEAD_DIM - a, :]
    sgw = r["sgw"]
    for k in range(nh):
        sgw[k] = padt[starts[k] : starts[k] + width, :].T
    ogt[...] = og_ref[...].astype(F32).T
    order = list(range(chunks))
    for c in order[:1:-1]:
        inner(c)

    def prefixes():
        early.wait_in()
        total = jnp.zeros_like(r["inbox"][0])
        for m in range(ns):
            r["outbox"][m] = total
            total = total + r["inbox"][m]
        early.start_out()

    early.own(prefixes)
    for c in order[1::-1]:
        inner(c)
    pairs = range(nh // 2)
    ends = starts[1:] + [PADDED]
    lane = lax.broadcasted_iota(jnp.int32, (HEAD_DIM, width), 1)

    def size_of(window):
        at = window_at(starts, window, nh)
        return window_at(ends, window, nh) - at

    def rows_of(window):
        return pl.ds(pl.multiple_of(window_at(starts, window, nh), 16), width)

    low = r["low"]

    def read_window(window):
        state = sgw[window] + r["carry"][window]
        low[...] = jnp.where(lane < size_of(window), state, 0.0).astype(BF16)

    def partial(window):
        read_window(window)
        rows = rows_of(window)
        for c in range(chunks):
            for k in range(heads):
                here = slice(k * HEAD_DIM, (k + 1) * HEAD_DIM)
                at = slice(c * CHUNK, (c + 1) * CHUNK)
                attt[here, at] += dot(low[...], f_all[c * heads + k, rows, :])

    for i in pairs:
        early.wait_out(i)
        early.side_copy(i, h).start()
        partial(lax.rem(h + 2 * i, nh))
    for i in pairs:
        early.side_copy(i, beside).wait_recv()
        if i < pairs[-1]:
            partial(lax.rem(beside + 2 * i, nh))
    last = lax.rem(beside + 2 * pairs[-1], nh)
    read_window(last)

    def normalize(c, _):
        at = pl.ds(pl.multiple_of(c * CHUNK, CHUNK), CHUNK)
        for k in range(heads):
            here = slice(k * HEAD_DIM, (k + 1) * HEAD_DIM)
            numer = attt[here, at] + dot(low[...], f_all[c * heads + k, rows_of(last), :])
            scale = lax.rsqrt(jnp.mean(numer * numer, axis=0, keepdims=True) + EPS)
            normed = numer * scale
            up = ogt[here, at]
            attt[here, at] = normed
            dn = (scale * (up - normed * jnp.mean(up * normed, axis=0, keepdims=True))).astype(BF16)
            dnt[here, at] = dn
        return 0

    lax.fori_loop(0, chunks, normalize, 0, unroll=True)

    near = r["near"]

    def state_window(window):
        rows = rows_of(window)
        sgw[window] = sum(
            dot(
                dnt[k * HEAD_DIM : (k + 1) * HEAD_DIM, c * CHUNK : (c + 1) * CHUNK],
                f_all[c * heads + k, rows, :],
                ((1,), (1,)),
            )
            for c in range(chunks)
            for k in range(heads)
        )

    def swap(i, head):
        window = lax.rem(head + 2 * i, nh)
        return push(
            sgw.at[window], near.at[window // 2], r["ns"].at[window // 2],
            r["nr"].at[window // 2], (s, beside),
        )

    mids = [r["mid"].at[i] for i in pairs]
    for i in pairs[::-1]:
        state_window(lax.rem(beside + 2 * i, nh))
        swap(i, beside).start()
    for i in pairs[::-1]:
        window = lax.rem(h + 2 * i, nh)
        state_window(window)
        swap(i, h).wait_recv()
        r["mid"][i] = sgw[window] + near[window // 2]
        late.start_in(mids[i], i)
    early.end_in([u_ref])
    early.own(early.end_out)
    for i in pairs:
        early.side_copy(i, h).wait_send()
    startt[...] = (padt[...] + joined(r["carry"], starts)).astype(BF16)
    kvl[...] = jnp.zeros_like(kvl)
    for c in order[:1:-1]:
        upward(c)
    core = lax.rem(h, 2)
    kvnear, kvfar, kvsum = r["kvnear"], r["kvfar"], r["kvsum"]

    def kv_swap(q, side):
        return push(
            kvl.at[block(2 * q + side, CHUNK), :], kvnear.at[q], r["kvs"].at[q], r["kvr"].at[q], (s, beside)
        )

    kv_swap(1, 1 - core).start()
    tot, win = r["tot"], r["win"]

    def total_copies():
        return [
            push(
                tot, win.at[block(late.rank, 8), :], r["ts"].at[k], r["tr"].at[late.rank],
                (lax.rem(s + k, ns), h),
            )
            for k in range(1, ns)
        ]

    def suffixes():
        late.wait_in()
        total = jnp.zeros_like(r["sinbox"][0])
        for m in reversed(range(ns)):
            r["soutbox"][m] = total
            for i in pairs:
                total = total + r["sinbox"][m * (nh // 2) + i]
        tot[...] = total
        late.start_out()
        for copy in total_copies():
            copy.start()
        win[block(late.rank, 8), :] = total

    late.own(suffixes)
    upward(1)
    kvacross = []

    def kv_across(q):
        kv_swap(q, 1 - core).wait()
        kvsum[q] = kvl[block(2 * q + core, CHUNK), :] + kvnear[q]
        for k in range(1, nh // 2):
            to = (s, lax.rem(h + 2 * k, nh))
            kvacross.append(links.copy(kvsum.at[q], kvfar.at[k - 1, q], to))
            kvacross[-1].start()

    kv_across(1)
    upward(0)
    kv_swap(0, 1 - core).start()
    kxs = r["kxs"]
    for c in range(chunks):
        at = slice(c * CHUNK, (c + 1) * CHUNK)
        kxs[c] = scaled(kvt[:HEAD_DIM, at])
        write_features(kvt.at[:HEAD_DIM, at], kxs.at[c], f_all.at[c], CHUNK)
    kv_across(0)
    att_ref, qg_ref = r["att"], r["qg"]
    att_ref[...] = attt[...].T.astype(BF16)
    qg_ref[...] = qgt[...].T.astype(BF16)
    for i in pairs:
        swap(i, beside).wait_send()
    part_ref, other_ref, kv_out = r["part"], r["other"], r["kv_grad"]

    def chunk_of(k, side):
        return 2 * (k % (chunks // 2)) + (1 - side if k < chunks // 2 else side)

    def side(k):
        c = chunk_of(k, core)
        return push(
            part_ref.at[c], other_ref.at[c], r["xs_send"].at[c], r["xs_recv"].at[c], (s, beside)
        )

    def key_chunk(k, w, first):
        c = chunk_of(k, core)
        at = pl.ds(pl.multiple_of(c * CHUNK, CHUNK), CHUNK)
        size = ends[w] - starts[w]
        df[starts[w] : ends[w], :] = dot(startt[starts[w] : ends[w], :], vt[:, at])
        seen = dot(low[...], f_all[c, starts[w] : starts[w] + width, :])
        ranges = [(starts[w], ends[w])]
        grad = jnp.concatenate([feature_grad(kxs.at[c], df, row, CHUNK, ranges), seen], axis=0).T
        part_ref[c] = grad if first else part_ref[c] + grad

    for i in pairs:
        late.wait_out(i)
        final = i == pairs[-1]
        if final:
            for copy in kvacross:
                copy.wait()
            for k in range(nh // 2 - 1):
                kvsum[...] += kvfar[k]
        for w in range(nh):
            @pl.when(lax.rem(h + 2 * i, nh) == w)
            def _(i=i, w=w):
                size = ends[w] - starts[w]
                state = r["later"][w]
                startt[starts[w] : ends[w], :] = state.T[:size].astype(BF16)
                low[...] = jnp.where(lane < size, state, 0.0).astype(BF16)
                for k in range(chunks):
                    key_chunk(k, w, i == 0)
                    if i == pairs[-1]:
                        if k >= chunks // 2:
                            part_ref[chunk_of(k, core)] += kvsum[k - chunks // 2]
                        side(k).start()
    late.end_in(mids)
    late.own(late.end_out)
    for k in range(late.groups):
        j = lax.rem(late.rank + k, late.groups)
        box = win.at[block(j, 8), :]
        copy = push(box, box, r["ts"].at[0], r["tr"].at[j], (s, beside))
        if k == 0:
            late.own(lambda: None, copy.wait_recv)
        else:
            copy.wait_recv()

    def end_totals():
        for copy in total_copies():
            copy.wait_send()

    late.own(end_totals)
    own_window = pl.ds(pl.multiple_of(window_at(starts, h, nh), 16), width)
    padt[own_window, :] = win[...].T
    canon = r["tall"]
    for a in range(HEAD_DIM):
        at = STARTS[a] + a % 8
        canon[CANON[a] : CANON[a] + HEAD_DIM - a, :] = padt[at : at + HEAD_DIM - a, :]
    slice_width = features // nh
    flip, init_out = r["flip"], r["init_grad"]
    flip[:slice_width, :] = canon[block(h, slice_width), :]
    init_out[...] = flip[...].T[:, :slice_width]
    for k in range(chunks):
        side(k).wait_send()
        c = chunk_of(k, 1 - core)
        copy = push(
            part_ref.at[c], other_ref.at[c], r["xs_send"].at[c], r["xs_recv"].at[c], (s, beside)
        )
        copy.wait_recv()
        kv_out[block(c, CHUNK), :] = part_ref[c] + other_ref[c]


def deliver_kernel(count, *refs):
    sems = refs[2 * count]
    copies = [
        pltpu.make_async_copy(refs[i], refs[count + i], sems.at[i]) for i in range(count)
    ]
    for copy in copies:
        copy.start()
    for copy in copies:
        copy.wait()


def deliver(arrays):
    here = pl.BlockSpec(memory_space=pl.ANY)
    return pl.pallas_call(
        functools.partial(deliver_kernel, len(arrays)),
        out_shape=tuple(jax.ShapeDtypeStruct(x.shape, x.dtype) for x in arrays),
        in_specs=[pl.BlockSpec(memory_space=pltpu.VMEM)] * len(arrays),
        out_specs=(here,) * len(arrays),
        scratch_shapes=[pltpu.SemaphoreType.DMA((len(arrays),))],
        compiler_params=pltpu.CompilerParams(vmem_limit_bytes=2 * 1024 * 1024),
    )(*arrays)


def per_device(ns, nh, queries, keys_values, init_state, out_grad):
    tokens, wide = queries.shape
    assert tokens == GROUP and ns % 8 == 0 and nh % 2 == 0 and tokens // nh == CHUNK
    features = init_state.shape[1]
    heads = wide // HEAD_DIM
    pair, groups = nh // 2, HEAD_DIM // 8
    even = -(-features // 128) * 128
    starts, width = windows(features, nh)
    slice_width = features // nh
    D, V = pltpu.SemaphoreType.DMA, pltpu.VMEM
    piece, window = (8, width), (HEAD_DIM, width)
    columns, chunk = (wide, tokens), (HEAD_DIM, CHUNK)
    count = 2 * (pair - 1)
    outs = dict(
        att=((tokens, wide), BF16),
        qg=((tokens, wide), BF16),
        kv_grad=((tokens, 2 * HEAD_DIM), F32),
        init_grad=((HEAD_DIM, slice_width), F32),
    )
    scratch = dict(
        kvt=V((2 * HEAD_DIM, tokens), F32), x=V(chunk, F32), xs=V(chunk, F32), row=V(chunk, F32),
        df=V((PADDED, CHUNK), F32), f=V((tokens // CHUNK * heads, PADDED, CHUNK), BF16),
        qt=V(columns, F32), ogt=V(columns, F32), attt=V(columns, F32), qgt=V(columns, F32),
        dnt=V(columns, BF16), startt=V((PADDED, HEAD_DIM), BF16),
        keys=V((tokens, HEAD_DIM), BF16), vals=V((tokens, HEAD_DIM), BF16),
        kt=V((HEAD_DIM, tokens), BF16), vt=V((HEAD_DIM, tokens), BF16),
        carry=V((nh,) + window, F32), later=V((nh,) + window, F32),
        kvl=V((tokens, 2 * HEAD_DIM), F32), padt=V((PADDED, HEAD_DIM), F32),
        tall=V((even, HEAD_DIM), F32), wide=V((HEAD_DIM, even), F32),
        u=V(window, F32), inbox=V((ns,) + piece, F32), outbox=V((ns,) + piece, F32),
        sinbox=V((ns * pair,) + piece, F32), soutbox=V((ns,) + piece, F32), tot=V(piece, F32),
        near=V((pair,) + window, F32), mid=V((pair,) + window, F32), sgw=V((nh,) + window, F32),
        kvnear=V((2, CHUNK, 2 * HEAD_DIM), F32), kvsum=V((2, CHUNK, 2 * HEAD_DIM), F32),
        kvfar=V((max(pair - 1, 1), 2, CHUNK, 2 * HEAD_DIM), F32),
        kxs=V((tokens // CHUNK,) + chunk, F32), win=V(window, F32),
        part=V((tokens // CHUNK, CHUNK, 2 * HEAD_DIM), F32),
        other=V((tokens // CHUNK, CHUNK, 2 * HEAD_DIM), F32),
        flip=V((-(-slice_width // 128) * 128, HEAD_DIM), F32),
        xs_send=D((tokens // CHUNK,)), xs_recv=D((tokens // CHUNK,)), kvs=D((2,)), kvr=D((2,)), low=V((HEAD_DIM, width), BF16),
        sends=D((count,)), recvs=D((count,)), ns=D((pair,)), nr=D((pair,)), ts=D((ns,)), tr=D((groups,)),
        ais=D((groups,)), air=D((ns,)), cis=D((groups * pair,)), cir=D((ns * pair,)),
    )
    scratch["ass"], scratch["asr"] = D((pair,)), D((pair,))
    for name in ("a", "c"):
        scratch[name + "os"], scratch[name + "or"] = D((ns * pair,)), D((groups * pair,))
    for c in range(tokens // CHUNK):
        scratch[f"logits{c}"] = V((heads, (c + 1) * CHUNK, CHUNK), F32)
        scratch[f"weights{c}"] = V((heads, (c + 1) * CHUNK, CHUNK), BF16)
    names = ["q", "kv", "init", "og"] + list(outs) + list(scratch)
    vmem = pl.BlockSpec(memory_space=pltpu.VMEM)
    results = pl.pallas_call(
        functools.partial(main_kernel, ns, nh, names, starts, width),
        out_shape=tuple(pltpu.VMEM(*out) for out in outs.values()),
        in_specs=[vmem] * 4,
        out_specs=(vmem,) * len(outs),
        scratch_shapes=list(scratch.values()),
        compiler_params=pltpu.CompilerParams(
            vmem_limit_bytes=60 * 1024 * 1024, collective_id=1, has_side_effects=True
        ),
    )(queries, keys_values, init_state, out_grad)
    return deliver(results)


def solution(mesh):
    ns, nh = mesh.shape["seq"], mesh.shape["head"]
    return jax.shard_map(
        functools.partial(per_device, ns, nh),
        mesh=mesh,
        in_specs=(P("seq", "head"), P("seq", None), P(), P("seq", "head")),
        out_specs=(P("seq", "head"), P("seq", "head"), P("seq", None), P(None, "head")),
        check_vma=False,
    )
```

```python
import functools

import jax
import jax.numpy as jnp
import numpy as np
from jax import lax
from jax.experimental import pallas as pl
from jax.experimental.pallas import tpu as pltpu
from jax.sharding import PartitionSpec as P

HEAD_DIM = 64
GROUP = 1024
EPS = 1e-06
CHUNK = 256
MESH = pl.DeviceIdType.MESH
F32, BF16 = jnp.float32, jnp.bfloat16


def padded_layout(width):
    starts, at = [], 0
    for a in range(width):
        starts.append(at)
        at += width - a // 8 * 8
    return starts, at


STARTS, PADDED = padded_layout(HEAD_DIM)
CANON = [a * HEAD_DIM - a * (a - 1) // 2 for a in range(HEAD_DIM)]


def dot(first, second, contract=((1,), (0,))):
    return lax.dot_general(first, second, (contract, ((), ())), preferred_element_type=F32)


def edge_weights(cols):
    row = lax.broadcasted_iota(jnp.int32, (8, cols), 0)
    return [
        jnp.where(row < m, 0.0, jnp.where(row == m, float(np.sqrt(0.5)), 1.0)).astype(F32)
        for m in range(8)
    ]


def write_features(x_ref, xs_ref, f_ref, cols):
    edges = edge_weights(cols)
    for a in range(0, HEAD_DIM, 2):
        base = a // 8 * 8
        parts = []
        for c in (a, a + 1):
            prod = x_ref[c : c + 1, :] * xs_ref[base:, :]
            parts.append(prod[:8] * edges[c % 8])
            if base + 8 < HEAD_DIM:
                parts.append(prod[8:])
        at = STARTS[a]
        f_ref[at : at + 2 * (HEAD_DIM - base), :] = jnp.concatenate(parts, axis=0).astype(BF16)


def write_window(x_ref, xs_ref, f_ref, cols, first, width):
    edges = edge_weights(cols)
    for a in range(0, HEAD_DIM, 2):
        base = a // 8 * 8
        at, end = STARTS[a], STARTS[a] + 2 * (HEAD_DIM - base)
        lo, hi = max(at, first), min(end, first + width)
        if lo >= hi:
            continue
        parts = []
        for c in (a, a + 1):
            prod = x_ref[c : c + 1, :] * xs_ref[base:, :]
            parts.append(prod[:8] * edges[c % 8])
            if base + 8 < HEAD_DIM:
                parts.append(prod[8:])
        rows = jnp.concatenate(parts, axis=0)[lo - at : hi - at]
        f_ref[lo - first : hi - first, :] = rows.astype(BF16)


def feature_grad(xs_ref, df_ref, row_ref, cols, ranges=((0, PADDED),)):
    edges = edge_weights(cols)
    tiles = HEAD_DIM // 8
    acc = [jnp.zeros((8, cols), F32) for _ in range(tiles)]
    for a in range(HEAD_DIM):
        first = a // 8
        xa = jnp.broadcast_to(xs_ref[a : a + 1, :], (8, cols))
        total = None
        for t in range(first, tiles):
            at = STARTS[a] + (t - first) * 8
            if not any(lo <= at < hi for lo, hi in ranges):
                continue
            part = df_ref[at : at + 8, :]
            if t == first:
                part = part * edges[a % 8]
            acc[t] = acc[t] + part * xa
            term = part * xs_ref[t * 8 : t * 8 + 8, :]
            total = term if total is None else total + term
        if total is None:
            total = jnp.zeros((8, cols), F32)
        row_ref[a : a + 1, :] = jnp.sum(total, axis=0, keepdims=True)
    return jnp.concatenate(acc, axis=0) + row_ref[...]


def scaled(x):
    return x * float(np.sqrt(2.0 / HEAD_DIM))


def places(ns, nh):
    s, h = lax.axis_index("seq"), lax.axis_index("head")
    beside = h + 1 - 2 * (h % 2)
    same = [
        (lax.rem(s + k, ns), lax.rem(h + 2 * i, nh))
        for k in range(ns)
        for i in range(nh // 2)
        if (k, i) != (0, 0)
    ]
    other = [(s, lax.rem(beside + 2 * i, nh)) for i in range(nh // 2)]
    return s, h, beside, same + other


def push(src, dst, send, recv, device):
    return pltpu.make_async_remote_copy(
        src_ref=src, dst_ref=dst, send_sem=send, recv_sem=recv,
        device_id=device, device_id_type=MESH,
    )


class Exchange:
    def __init__(self, ns, nh, s, h, beside, heads_in, inbox, outbox, landed, sems):
        self.ns, self.nh, self.s, self.h, self.beside = ns, nh, s, h, beside
        self.groups = HEAD_DIM // 8
        self.step = ns // self.groups
        self.rank, self.pair, self.lane = s // self.step, nh // 2, h // 2
        self.heads_in, self.inbox, self.outbox, self.landed = heads_in, inbox, outbox, landed
        self.in_send, self.in_recv, self.out_send, self.out_recv = sems[:4]
        self.side = sems[4:]

    def own(self, then, otherwise=None):
        if self.step == 1:
            then()
            return
        mine = lax.rem(self.s, self.step) == 0
        pl.when(mine)(then)
        if otherwise is not None:
            pl.when(jnp.logical_not(mine))(otherwise)

    def in_slot(self, k, i):
        at = lax.rem(self.s + k, self.ns)
        return at * self.heads_in + (lax.rem(self.lane + i, self.pair) if self.heads_in > 1 else 0)

    def in_copy(self, piece, i, k):
        to = (lax.rem(self.rank + k, self.groups), lax.rem(self.h + 2 * i, self.nh))
        slot = self.in_slot(0, 0)
        return push(
            piece.at[block(to[0], 8), :], self.inbox.at[slot], self.in_send.at[i * self.groups + k],
            self.in_recv.at[slot], (to[0] * self.step, to[1]),
        )

    def start_in(self, piece, i=0):
        for k in range(1, self.groups + 1):
            copy = self.in_copy(piece, i, k % self.groups)
            if i == 0 and k == self.groups:
                self.own(lambda: self.keep(piece), copy.start)
            else:
                copy.start()

    def keep(self, piece):
        self.inbox[self.in_slot(0, 0)] = piece[block(self.rank, 8), :]

    def end_in(self, pieces):
        for i, piece in enumerate(pieces):
            for k in range(self.groups):
                copy = self.in_copy(piece, i, k)
                if i == 0 and k == 0:
                    self.own(lambda: None, copy.wait_send)
                else:
                    copy.wait_send()

    def wait_in(self):
        for k in range(self.ns):
            for i in range(self.heads_in):
                if (k, i) != (0, 0):
                    slot = self.in_slot(k, i)
                    box = self.inbox.at[slot]
                    push(box, box, self.in_send.at[0], self.in_recv.at[slot], (self.s, self.beside)).wait_recv()

    def out_copies(self):
        made = []
        for i in range(self.pair):
            for k in range(self.ns):
                n = lax.rem(self.s + k, self.ns)
                if (k, i) != (0, 0):
                    made.append(push(
                        self.outbox.at[n], self.landed.at[self.h, block(self.rank, 8), :],
                        self.out_send.at[k * self.pair + i],
                        self.out_recv.at[self.rank * self.pair + self.lane],
                        (n, lax.rem(self.h + 2 * i, self.nh)),
                    ))
        return made

    def start_out(self):
        for copy in self.out_copies():
            copy.start()
        self.landed[self.h, block(self.rank, 8), :] = self.outbox[self.s]

    def end_out(self):
        for copy in self.out_copies():
            copy.wait_send()

    def wait_out(self, i):
        window = lax.rem(self.h + 2 * i, self.nh)
        for k in range(self.groups):
            j, lane = lax.rem(self.rank + k, self.groups), window // 2
            box = self.landed.at[window, block(j, 8), :]
            copy = push(
                box, box, self.out_send.at[0], self.out_recv.at[j * self.pair + lane], (self.s, self.beside)
            )
            if (k, i) == (0, 0):
                self.own(lambda: None, copy.wait_recv)
            else:
                copy.wait_recv()

    def side_copy(self, i, head):
        window = lax.rem(head + 2 * i, self.nh)
        box = self.landed.at[window]
        return push(
            box, box, self.side[0].at[window // 2], self.side[1].at[window // 2], (self.s, self.beside)
        )


def block(index, size):
    return pl.ds(pl.multiple_of(index * size, 8), size)


class Links:
    def __init__(self, sends, recvs):
        self.sends, self.recvs, self.used = sends, recvs, 0

    def copy(self, src, dst, device):
        k = self.used
        self.used += 1
        return pltpu.make_async_remote_copy(
            src_ref=src, dst_ref=dst, send_sem=self.sends.at[k], recv_sem=self.recvs.at[k],
            device_id=device, device_id_type=MESH,
        )


def padded_column(c):
    a = max(a for a in range(HEAD_DIM) if CANON[a] <= c)
    return STARTS[a] + a % 8 + c - CANON[a]


def windows(features, nh):
    wide = features // nh
    ends = [(padded_column(k * wide), padded_column(k * wide + wide - 1)) for k in range(nh)]
    starts = [lo // 16 * 16 for lo, _ in ends]
    width = max(-(-(hi + 1 - lo) // 128) * 128 for lo, (_, hi) in zip(starts, ends))
    starts = [min(lo, PADDED - width) for lo in starts]
    assert starts[0] == 0 and all(b - a <= width for a, b in zip(starts, starts[1:]))
    return starts, width


def joined(landed, starts):
    ends = starts[1:] + [PADDED]
    return jnp.concatenate(
        [landed[k].T[: ends[k] - starts[k]] for k in range(len(starts))], axis=0
    )


def window_at(starts, owner, nh):
    at = starts[0]
    for k in range(1, nh):
        at = at + (starts[k] - starts[k - 1]) * ((owner + nh - k) // nh)
    return at


def masked(full, causal):
    n = full.shape[0]
    last = jnp.where(causal, full[n - CHUNK :], 0.0)
    if n == CHUNK:
        return last.astype(BF16)
    return jnp.concatenate([full[: n - CHUNK], last], axis=0).astype(BF16)


def main_kernel(ns, nh, names, starts, width, *refs):
    r = dict(zip(names, refs))
    q_ref, kv_ref, init_ref, og_ref = r["q"], r["kv"], r["init"], r["og"]
    kvt, xs, x, row, df, f_all = r["kvt"], r["xs"], r["x"], r["row"], r["df"], r["f"]
    qt, ogt, attt, qgt, dnt = r["qt"], r["ogt"], r["attt"], r["qgt"], r["dnt"]
    startt, keys, vals, kt, vt = r["startt"], r["keys"], r["vals"], r["kt"], r["vt"]
    kvl = r["kvl"]
    padt, tall = r["padt"], r["tall"]
    tokens = q_ref.shape[0]
    heads = q_ref.shape[1] // HEAD_DIM
    chunks = tokens // CHUNK
    features = init_ref.shape[1]
    s, h, beside, peers = places(ns, nh)
    links = Links(r["sends"], r["recvs"])
    sems = lambda name: [r[name + x] for x in ("is", "ir", "os", "or", "ss", "sr") if name + x in r]
    early = Exchange(ns, nh, s, h, beside, 1, r["inbox"], r["outbox"], r["carry"], sems("a"))
    late = Exchange(ns, nh, s, h, beside, nh // 2, r["sinbox"], r["soutbox"], r["later"], sems("c"))
    loads = [
        pltpu.make_async_copy(r[name], r[name + "_in"], r["loads"].at[i])
        for i, name in enumerate(("q", "init", "og"))
    ]
    for load in loads:
        load.start()
    barrier = pltpu.get_barrier_semaphore()
    for device in peers:
        pl.semaphore_signal(barrier, inc=1, device_id=device, device_id_type=MESH)

    kvt[...] = kv_ref[...].astype(F32).T
    vt[...] = kvt[HEAD_DIM:, :].astype(BF16)
    u_ref = r["u"]
    for c in range(chunks):
        at = slice(c * CHUNK, (c + 1) * CHUNK)
        xs[...] = scaled(kvt[:HEAD_DIM, at])
        for k in range(nh):
            @pl.when(h == k)
            def _(c=c, at=at, k=k):
                write_window(kvt.at[:HEAD_DIM, at], xs, f_all.at[c], CHUNK, starts[k], width)
    u_ref[...] = sum(
        dot(vt[:, c * CHUNK : (c + 1) * CHUNK], f_all[c, :width, :], ((1,), (1,)))
        for c in range(chunks)
    )
    pl.semaphore_wait(barrier, len(peers))
    early.start_in(u_ref)
    for load in loads:
        load.wait()

    qt[...] = r["q_in"][...].astype(F32).T
    kt[...] = kvt[:HEAD_DIM, :].astype(BF16)
    keys[...] = kv_ref[:, :HEAD_DIM]
    vals[...] = kv_ref[:, HEAD_DIM:]
    causal = lax.broadcasted_iota(jnp.int32, (CHUNK, CHUNK), 0) <= lax.broadcasted_iota(
        jnp.int32, (CHUNK, CHUNK), 1
    )

    def inner(c):
        n = (c + 1) * CHUNK
        at = slice(c * CHUNK, n)

        def one_head(k, _):
            here = pl.ds(pl.multiple_of(k * HEAD_DIM, HEAD_DIM), HEAD_DIM)
            query = qt[here, at]
            x[...] = query
            xs[...] = scaled(query)
            write_features(x, xs, f_all.at[c * heads + k], CHUNK)
            logits = dot(keys[:n], query.astype(BF16))
            weights = masked(logits * logits * (1.0 / HEAD_DIM), causal)
            r[f"logits{c}"][k] = logits
            r[f"weights{c}"][k] = weights
            attt[here, at] = dot(vt[:, :n], weights)
            return 0

        lax.fori_loop(0, heads, one_head, 0)

    def upward(c):
        n = (c + 1) * CHUNK
        at = slice(c * CHUNK, n)

        def one_head(k, _):
            here = pl.ds(pl.multiple_of(k * HEAD_DIM, HEAD_DIM), HEAD_DIM)
            query = qt[here, at]
            xs[...] = scaled(query)
            dn = dnt[here, at]
            df[...] = dot(startt[...], dn)
            dw = dot(vals[:n], dn)
            dl = masked(dw * r[f"logits{c}"][k] * (2.0 / HEAD_DIM), causal)
            qgt[here, at] = dot(kt[:, :n], dl) + feature_grad(xs, df, row, CHUNK)
            kvl[:n, :HEAD_DIM] += dot(dl, query.astype(BF16), ((1,), (1,)))
            kvl[:n, HEAD_DIM:] += dot(r[f"weights{c}"][k], dn, ((1,), (1,)))
            return 0

        lax.fori_loop(0, heads, one_head, 0, unroll=True)

    wide = r["wide"]
    whole_lanes = features // 128 * 128
    padt[...] = jnp.zeros_like(padt)
    wide[:, whole_lanes:] = jnp.zeros_like(wide[:, whole_lanes:])
    wide[:, :features] = r["init_in"][...]
    tall[...] = wide[...].T
    for a in range(HEAD_DIM):
        at = STARTS[a] + a % 8
        padt[at : at + HEAD_DIM - a, :] = tall[CANON[a] : CANON[a] + HEAD_DIM - a, :]
    sgw = r["sgw"]
    for k in range(nh):
        sgw[k] = padt[starts[k] : starts[k] + width, :].T
    ogt[...] = r["og_in"][...].astype(F32).T
    order = list(range(chunks))
    for c in order[:1:-1]:
        inner(c)

    def prefixes():
        early.wait_in()
        total = jnp.zeros_like(r["inbox"][0])
        for m in range(ns):
            r["outbox"][m] = total
            total = total + r["inbox"][m]
        early.start_out()

    early.own(prefixes)
    for c in order[1::-1]:
        inner(c)
    pairs = range(nh // 2)
    ends = starts[1:] + [PADDED]
    lane = lax.broadcasted_iota(jnp.int32, (HEAD_DIM, width), 1)

    def size_of(window):
        at = window_at(starts, window, nh)
        return window_at(ends, window, nh) - at

    def rows_of(window):
        return pl.ds(pl.multiple_of(window_at(starts, window, nh), 16), width)

    low = r["low"]

    def read_window(window):
        state = sgw[window] + r["carry"][window]
        low[...] = jnp.where(lane < size_of(window), state, 0.0).astype(BF16)

    def partial(window):
        read_window(window)
        rows = rows_of(window)
        for c in range(chunks):
            for k in range(heads):
                here = slice(k * HEAD_DIM, (k + 1) * HEAD_DIM)
                at = slice(c * CHUNK, (c + 1) * CHUNK)
                attt[here, at] += dot(low[...], f_all[c * heads + k, rows, :])

    for i in pairs:
        early.wait_out(i)
        early.side_copy(i, h).start()
        partial(lax.rem(h + 2 * i, nh))
    for i in pairs:
        early.side_copy(i, beside).wait_recv()
        if i < pairs[-1]:
            partial(lax.rem(beside + 2 * i, nh))
    last = lax.rem(beside + 2 * pairs[-1], nh)
    read_window(last)

    def normalize(c, _):
        at = pl.ds(pl.multiple_of(c * CHUNK, CHUNK), CHUNK)
        for k in range(heads):
            here = slice(k * HEAD_DIM, (k + 1) * HEAD_DIM)
            numer = attt[here, at] + dot(low[...], f_all[c * heads + k, rows_of(last), :])
            scale = lax.rsqrt(jnp.mean(numer * numer, axis=0, keepdims=True) + EPS)
            normed = numer * scale
            up = ogt[here, at]
            attt[here, at] = normed
            dn = (scale * (up - normed * jnp.mean(up * normed, axis=0, keepdims=True))).astype(BF16)
            dnt[here, at] = dn
        return 0

    lax.fori_loop(0, chunks, normalize, 0, unroll=True)

    near = r["near"]

    def state_window(window):
        rows = rows_of(window)
        sgw[window] = sum(
            dot(
                f_all[c * heads + k, rows, :],
                dnt[k * HEAD_DIM : (k + 1) * HEAD_DIM, c * CHUNK : (c + 1) * CHUNK],
                ((1,), (1,)),
            )
            for c in range(chunks)
            for k in range(heads)
        ).T

    def swap(i, head):
        window = lax.rem(head + 2 * i, nh)
        return push(
            sgw.at[window], near.at[window // 2], r["ns"].at[window // 2],
            r["nr"].at[window // 2], (s, beside),
        )

    mids = [r["mid"].at[i] for i in pairs]
    for i in pairs[::-1]:
        state_window(lax.rem(beside + 2 * i, nh))
        swap(i, beside).start()
    for i in pairs[::-1]:
        window = lax.rem(h + 2 * i, nh)
        state_window(window)
        swap(i, h).wait_recv()
        r["mid"][i] = sgw[window] + near[window // 2]
        late.start_in(mids[i], i)
    early.end_in([u_ref])
    early.own(early.end_out)
    for i in pairs:
        early.side_copy(i, h).wait_send()
    startt[...] = (padt[...] + joined(r["carry"], starts)).astype(BF16)
    kvl[...] = jnp.zeros_like(kvl)
    for c in order[:1:-1]:
        upward(c)
    core = lax.rem(h, 2)
    kvnear, kvfar, kvsum = r["kvnear"], r["kvfar"], r["kvsum"]

    def kv_swap(q, side):
        return push(
            kvl.at[block(2 * q + side, CHUNK), :], kvnear.at[q], r["kvs"].at[q], r["kvr"].at[q], (s, beside)
        )

    kv_swap(1, 1 - core).start()
    tot, win = r["tot"], r["win"]

    def total_copies():
        return [
            push(
                tot, win.at[block(late.rank, 8), :], r["ts"].at[k], r["tr"].at[late.rank],
                (lax.rem(s + k, ns), h),
            )
            for k in range(1, ns)
        ]

    def suffixes():
        late.wait_in()
        total = jnp.zeros_like(r["sinbox"][0])
        for m in reversed(range(ns)):
            r["soutbox"][m] = total
            for i in pairs:
                total = total + r["sinbox"][m * (nh // 2) + i]
        tot[...] = total
        late.start_out()
        for copy in total_copies():
            copy.start()
        win[block(late.rank, 8), :] = total

    late.own(suffixes)
    upward(1)
    kvacross = []

    def kv_across(q):
        kv_swap(q, 1 - core).wait()
        kvsum[q] = kvl[block(2 * q + core, CHUNK), :] + kvnear[q]
        for k in range(1, nh // 2):
            to = (s, lax.rem(h + 2 * k, nh))
            kvacross.append(links.copy(kvsum.at[q], kvfar.at[k - 1, q], to))
            kvacross[-1].start()

    kv_across(1)
    upward(0)
    kv_swap(0, 1 - core).start()
    kxs = r["kxs"]
    for c in range(chunks):
        at = slice(c * CHUNK, (c + 1) * CHUNK)
        kxs[c] = scaled(kvt[:HEAD_DIM, at])
        write_features(kvt.at[:HEAD_DIM, at], kxs.at[c], f_all.at[c], CHUNK)
    kv_across(0)
    att_ref, qg_ref = r["att"], r["qg"]
    att_ref[...] = attt[...].T.astype(BF16)
    qg_ref[...] = qgt[...].T.astype(BF16)
    for i in pairs:
        swap(i, beside).wait_send()
    part_ref, other_ref, kv_out = r["part"], r["other"], r["kv_grad"]

    def chunk_of(k, side):
        return 2 * (k % (chunks // 2)) + (1 - side if k < chunks // 2 else side)

    def side(k):
        c = chunk_of(k, core)
        return push(
            part_ref.at[c], other_ref.at[c], r["xs_send"].at[c], r["xs_recv"].at[c], (s, beside)
        )

    def key_chunk(k, w, first):
        c = chunk_of(k, core)
        at = pl.ds(pl.multiple_of(c * CHUNK, CHUNK), CHUNK)
        size = ends[w] - starts[w]
        df[starts[w] : ends[w], :] = dot(startt[starts[w] : ends[w], :], vt[:, at])
        seen = dot(low[...], f_all[c, starts[w] : starts[w] + width, :])
        ranges = [(starts[w], ends[w])]
        grad = jnp.concatenate([feature_grad(kxs.at[c], df, row, CHUNK, ranges), seen], axis=0).T
        part_ref[c] = grad if first else part_ref[c] + grad

    for i in pairs:
        late.wait_out(i)
        final = i == pairs[-1]
        if final:
            for copy in kvacross:
                copy.wait()
            for k in range(nh // 2 - 1):
                kvsum[...] += kvfar[k]
        for w in range(nh):
            @pl.when(lax.rem(h + 2 * i, nh) == w)
            def _(i=i, w=w):
                size = ends[w] - starts[w]
                state = r["later"][w]
                startt[starts[w] : ends[w], :] = state.T[:size].astype(BF16)
                low[...] = jnp.where(lane < size, state, 0.0).astype(BF16)
                for k in range(chunks):
                    key_chunk(k, w, i == 0)
                    if i == pairs[-1]:
                        if k >= chunks // 2:
                            part_ref[chunk_of(k, core)] += kvsum[k - chunks // 2]
                        side(k).start()
    late.end_in(mids)
    late.own(late.end_out)
    for k in range(late.groups):
        j = lax.rem(late.rank + k, late.groups)
        box = win.at[block(j, 8), :]
        copy = push(box, box, r["ts"].at[0], r["tr"].at[j], (s, beside))
        if k == 0:
            late.own(lambda: None, copy.wait_recv)
        else:
            copy.wait_recv()

    def end_totals():
        for copy in total_copies():
            copy.wait_send()

    late.own(end_totals)
    own_window = pl.ds(pl.multiple_of(window_at(starts, h, nh), 16), width)
    padt[own_window, :] = win[...].T
    canon = r["tall"]
    for a in range(HEAD_DIM):
        at = STARTS[a] + a % 8
        canon[CANON[a] : CANON[a] + HEAD_DIM - a, :] = padt[at : at + HEAD_DIM - a, :]
    slice_width = features // nh
    flip, init_out = r["flip"], r["init_grad"]
    flip[:slice_width, :] = canon[block(h, slice_width), :]
    init_out[...] = flip[...].T[:, :slice_width]
    for k in range(chunks):
        side(k).wait_send()
        c = chunk_of(k, 1 - core)
        copy = push(
            part_ref.at[c], other_ref.at[c], r["xs_send"].at[c], r["xs_recv"].at[c], (s, beside)
        )
        copy.wait_recv()
        kv_out[block(c, CHUNK), :] = part_ref[c] + other_ref[c]


def deliver_kernel(count, *refs):
    sems = refs[2 * count]
    copies = [
        pltpu.make_async_copy(refs[i], refs[count + i], sems.at[i]) for i in range(count)
    ]
    for copy in copies:
        copy.start()
    for copy in copies:
        copy.wait()


def deliver(arrays):
    here = pl.BlockSpec(memory_space=pl.ANY)
    return pl.pallas_call(
        functools.partial(deliver_kernel, len(arrays)),
        out_shape=tuple(jax.ShapeDtypeStruct(x.shape, x.dtype) for x in arrays),
        in_specs=[pl.BlockSpec(memory_space=pltpu.VMEM)] * len(arrays),
        out_specs=(here,) * len(arrays),
        scratch_shapes=[pltpu.SemaphoreType.DMA((len(arrays),))],
        compiler_params=pltpu.CompilerParams(vmem_limit_bytes=2 * 1024 * 1024),
    )(*arrays)


def per_device(ns, nh, queries, keys_values, init_state, out_grad):
    tokens, wide = queries.shape
    assert tokens == GROUP and ns % 8 == 0 and nh % 2 == 0 and tokens // nh == CHUNK
    features = init_state.shape[1]
    heads = wide // HEAD_DIM
    pair, groups = nh // 2, HEAD_DIM // 8
    even = -(-features // 128) * 128
    starts, width = windows(features, nh)
    slice_width = features // nh
    D, V = pltpu.SemaphoreType.DMA, pltpu.VMEM
    piece, window = (8, width), (HEAD_DIM, width)
    columns, chunk = (wide, tokens), (HEAD_DIM, CHUNK)
    count = 2 * (pair - 1)
    outs = dict(
        att=((tokens, wide), BF16),
        qg=((tokens, wide), BF16),
        kv_grad=((tokens, 2 * HEAD_DIM), F32),
        init_grad=((HEAD_DIM, slice_width), F32),
    )
    scratch = dict(
        q_in=V(queries.shape, BF16), init_in=V(init_state.shape, F32), og_in=V(out_grad.shape, BF16),
        loads=D((3,)), kvt=V((2 * HEAD_DIM, tokens), F32), x=V(chunk, F32), xs=V(chunk, F32), row=V(chunk, F32),
        df=V((PADDED, CHUNK), F32), f=V((tokens // CHUNK * heads, PADDED, CHUNK), BF16),
        qt=V(columns, F32), ogt=V(columns, F32), attt=V(columns, F32), qgt=V(columns, F32),
        dnt=V(columns, BF16), startt=V((PADDED, HEAD_DIM), BF16),
        keys=V((tokens, HEAD_DIM), BF16), vals=V((tokens, HEAD_DIM), BF16),
        kt=V((HEAD_DIM, tokens), BF16), vt=V((HEAD_DIM, tokens), BF16),
        carry=V((nh,) + window, F32), later=V((nh,) + window, F32),
        kvl=V((tokens, 2 * HEAD_DIM), F32), padt=V((PADDED, HEAD_DIM), F32),
        tall=V((even, HEAD_DIM), F32), wide=V((HEAD_DIM, even), F32),
        u=V(window, F32), inbox=V((ns,) + piece, F32), outbox=V((ns,) + piece, F32),
        sinbox=V((ns * pair,) + piece, F32), soutbox=V((ns,) + piece, F32), tot=V(piece, F32),
        near=V((pair,) + window, F32), mid=V((pair,) + window, F32), sgw=V((nh,) + window, F32),
        kvnear=V((2, CHUNK, 2 * HEAD_DIM), F32), kvsum=V((2, CHUNK, 2 * HEAD_DIM), F32),
        kvfar=V((max(pair - 1, 1), 2, CHUNK, 2 * HEAD_DIM), F32),
        kxs=V((tokens // CHUNK,) + chunk, F32), win=V(window, F32),
        part=V((tokens // CHUNK, CHUNK, 2 * HEAD_DIM), F32),
        other=V((tokens // CHUNK, CHUNK, 2 * HEAD_DIM), F32),
        flip=V((-(-slice_width // 128) * 128, HEAD_DIM), F32),
        xs_send=D((tokens // CHUNK,)), xs_recv=D((tokens // CHUNK,)), kvs=D((2,)), kvr=D((2,)), low=V((HEAD_DIM, width), BF16),
        sends=D((count,)), recvs=D((count,)), ns=D((pair,)), nr=D((pair,)), ts=D((ns,)), tr=D((groups,)),
        ais=D((groups,)), air=D((ns,)), cis=D((groups * pair,)), cir=D((ns * pair,)),
    )
    scratch["ass"], scratch["asr"] = D((pair,)), D((pair,))
    for name in ("a", "c"):
        scratch[name + "os"], scratch[name + "or"] = D((ns * pair,)), D((groups * pair,))
    for c in range(tokens // CHUNK):
        scratch[f"logits{c}"] = V((heads, (c + 1) * CHUNK, CHUNK), F32)
        scratch[f"weights{c}"] = V((heads, (c + 1) * CHUNK, CHUNK), BF16)
    names = ["q", "kv", "init", "og"] + list(outs) + list(scratch)
    vmem, far = pl.BlockSpec(memory_space=pltpu.VMEM), pl.BlockSpec(memory_space=pltpu.HBM)
    results = pl.pallas_call(
        functools.partial(main_kernel, ns, nh, names, starts, width),
        out_shape=tuple(pltpu.VMEM(*out) for out in outs.values()),
        in_specs=[far, vmem, far, far],
        out_specs=(vmem,) * len(outs),
        scratch_shapes=list(scratch.values()),
        compiler_params=pltpu.CompilerParams(
            vmem_limit_bytes=60 * 1024 * 1024, collective_id=1, has_side_effects=True
        ),
    )(queries, keys_values, init_state, out_grad)
    return deliver(results)


def solution(mesh):
    ns, nh = mesh.shape["seq"], mesh.shape["head"]
    return jax.shard_map(
        functools.partial(per_device, ns, nh),
        mesh=mesh,
        in_specs=(P("seq", "head"), P("seq", None), P(), P("seq", "head")),
        out_specs=(P("seq", "head"), P("seq", "head"), P("seq", None), P(None, "head")),
        check_vma=False,
    )
```

```python
import functools

import jax
import jax.numpy as jnp
import numpy as np
from jax import lax
from jax.experimental import pallas as pl
from jax.experimental.pallas import tpu as pltpu
from jax.sharding import PartitionSpec as P

HEAD_DIM = 64
GROUP = 1024
EPS = 1e-06
CHUNK = 256
MESH = pl.DeviceIdType.MESH
F32, BF16 = jnp.float32, jnp.bfloat16


def padded_layout(width):
    starts, at = [], 0
    for a in range(width):
        starts.append(at)
        at += width - a // 8 * 8
    return starts, at


STARTS, PADDED = padded_layout(HEAD_DIM)
CANON = [a * HEAD_DIM - a * (a - 1) // 2 for a in range(HEAD_DIM)]


def dot(first, second, contract=((1,), (0,))):
    return lax.dot_general(first, second, (contract, ((), ())), preferred_element_type=F32)


def edge_weights(cols):
    row = lax.broadcasted_iota(jnp.int32, (8, cols), 0)
    return [
        jnp.where(row < m, 0.0, jnp.where(row == m, float(np.sqrt(0.5)), 1.0)).astype(F32)
        for m in range(8)
    ]


def write_features(x_ref, xs_ref, f_ref, cols):
    edges = edge_weights(cols)
    for a in range(0, HEAD_DIM, 2):
        base = a // 8 * 8
        parts = []
        for c in (a, a + 1):
            prod = x_ref[c : c + 1, :] * xs_ref[base:, :]
            parts.append(prod[:8] * edges[c % 8])
            if base + 8 < HEAD_DIM:
                parts.append(prod[8:])
        at = STARTS[a]
        f_ref[at : at + 2 * (HEAD_DIM - base), :] = jnp.concatenate(parts, axis=0).astype(BF16)


def write_window(x_ref, xs_ref, f_ref, cols, first, width):
    edges = edge_weights(cols)
    for a in range(0, HEAD_DIM, 2):
        base = a // 8 * 8
        at, end = STARTS[a], STARTS[a] + 2 * (HEAD_DIM - base)
        lo, hi = max(at, first), min(end, first + width)
        if lo >= hi:
            continue
        parts = []
        for c in (a, a + 1):
            prod = x_ref[c : c + 1, :] * xs_ref[base:, :]
            parts.append(prod[:8] * edges[c % 8])
            if base + 8 < HEAD_DIM:
                parts.append(prod[8:])
        rows = jnp.concatenate(parts, axis=0)[lo - at : hi - at]
        f_ref[lo - first : hi - first, :] = rows.astype(BF16)


def feature_grad(xs_ref, df_ref, row_ref, cols, ranges=((0, PADDED),)):
    edges = edge_weights(cols)
    tiles = HEAD_DIM // 8
    acc = [jnp.zeros((8, cols), F32) for _ in range(tiles)]
    for a in range(HEAD_DIM):
        first = a // 8
        xa = jnp.broadcast_to(xs_ref[a : a + 1, :], (8, cols))
        total = None
        for t in range(first, tiles):
            at = STARTS[a] + (t - first) * 8
            if not any(lo <= at < hi for lo, hi in ranges):
                continue
            part = df_ref[at : at + 8, :]
            if t == first:
                part = part * edges[a % 8]
            acc[t] = acc[t] + part * xa
            term = part * xs_ref[t * 8 : t * 8 + 8, :]
            total = term if total is None else total + term
        if total is None:
            total = jnp.zeros((8, cols), F32)
        row_ref[a : a + 1, :] = jnp.sum(total, axis=0, keepdims=True)
    return jnp.concatenate(acc, axis=0) + row_ref[...]


def scaled(x):
    return x * float(np.sqrt(2.0 / HEAD_DIM))


def places(ns, nh):
    s, h = lax.axis_index("seq"), lax.axis_index("head")
    beside = h + 1 - 2 * (h % 2)
    same = [
        (lax.rem(s + k, ns), lax.rem(h + 2 * i, nh))
        for k in range(ns)
        for i in range(nh // 2)
        if (k, i) != (0, 0)
    ]
    other = [(s, lax.rem(beside + 2 * i, nh)) for i in range(nh // 2)]
    return s, h, beside, same + other


def push(src, dst, send, recv, device):
    return pltpu.make_async_remote_copy(
        src_ref=src, dst_ref=dst, send_sem=send, recv_sem=recv,
        device_id=device, device_id_type=MESH,
    )


class Exchange:
    def __init__(self, ns, nh, s, h, beside, heads_in, inbox, outbox, landed, sems):
        self.ns, self.nh, self.s, self.h, self.beside = ns, nh, s, h, beside
        self.groups = HEAD_DIM // 8
        self.step = ns // self.groups
        self.rank, self.pair, self.lane = s // self.step, nh // 2, h // 2
        self.heads_in, self.inbox, self.outbox, self.landed = heads_in, inbox, outbox, landed
        self.in_send, self.in_recv, self.out_send, self.out_recv = sems[:4]
        self.side = sems[4:]

    def own(self, then, otherwise=None):
        if self.step == 1:
            then()
            return
        mine = lax.rem(self.s, self.step) == 0
        pl.when(mine)(then)
        if otherwise is not None:
            pl.when(jnp.logical_not(mine))(otherwise)

    def in_slot(self, k, i):
        at = lax.rem(self.s + k, self.ns)
        return at * self.heads_in + (lax.rem(self.lane + i, self.pair) if self.heads_in > 1 else 0)

    def in_copy(self, piece, i, k):
        to = (lax.rem(self.rank + k, self.groups), lax.rem(self.h + 2 * i, self.nh))
        slot = self.in_slot(0, 0)
        return push(
            piece.at[block(to[0], 8), :], self.inbox.at[slot], self.in_send.at[i * self.groups + k],
            self.in_recv.at[slot], (to[0] * self.step, to[1]),
        )

    def start_in(self, piece, i=0):
        for k in range(1, self.groups + 1):
            copy = self.in_copy(piece, i, k % self.groups)
            if i == 0 and k == self.groups:
                self.own(lambda: self.keep(piece), copy.start)
            else:
                copy.start()

    def keep(self, piece):
        self.inbox[self.in_slot(0, 0)] = piece[block(self.rank, 8), :]

    def end_in(self, pieces):
        for i, piece in enumerate(pieces):
            for k in range(self.groups):
                copy = self.in_copy(piece, i, k)
                if i == 0 and k == 0:
                    self.own(lambda: None, copy.wait_send)
                else:
                    copy.wait_send()

    def wait_in(self):
        for k in range(self.ns):
            for i in range(self.heads_in):
                if (k, i) != (0, 0):
                    slot = self.in_slot(k, i)
                    box = self.inbox.at[slot]
                    push(box, box, self.in_send.at[0], self.in_recv.at[slot], (self.s, self.beside)).wait_recv()

    def out_copies(self):
        made = []
        for i in range(self.pair):
            for k in range(self.ns):
                n = lax.rem(self.s + k, self.ns)
                if (k, i) != (0, 0):
                    made.append(push(
                        self.outbox.at[n], self.landed.at[self.h, block(self.rank, 8), :],
                        self.out_send.at[k * self.pair + i],
                        self.out_recv.at[self.rank * self.pair + self.lane],
                        (n, lax.rem(self.h + 2 * i, self.nh)),
                    ))
        return made

    def start_out(self):
        for copy in self.out_copies():
            copy.start()
        self.landed[self.h, block(self.rank, 8), :] = self.outbox[self.s]

    def end_out(self):
        for copy in self.out_copies():
            copy.wait_send()

    def wait_out(self, i):
        window = lax.rem(self.h + 2 * i, self.nh)
        for k in range(self.groups):
            j, lane = lax.rem(self.rank + k, self.groups), window // 2
            box = self.landed.at[window, block(j, 8), :]
            copy = push(
                box, box, self.out_send.at[0], self.out_recv.at[j * self.pair + lane], (self.s, self.beside)
            )
            if (k, i) == (0, 0):
                self.own(lambda: None, copy.wait_recv)
            else:
                copy.wait_recv()

    def side_copy(self, i, head):
        window = lax.rem(head + 2 * i, self.nh)
        box = self.landed.at[window]
        return push(
            box, box, self.side[0].at[window // 2], self.side[1].at[window // 2], (self.s, self.beside)
        )


def block(index, size):
    return pl.ds(pl.multiple_of(index * size, 8), size)


class Links:
    def __init__(self, sends, recvs):
        self.sends, self.recvs, self.used = sends, recvs, 0

    def copy(self, src, dst, device):
        k = self.used
        self.used += 1
        return pltpu.make_async_remote_copy(
            src_ref=src, dst_ref=dst, send_sem=self.sends.at[k], recv_sem=self.recvs.at[k],
            device_id=device, device_id_type=MESH,
        )


def padded_column(c):
    a = max(a for a in range(HEAD_DIM) if CANON[a] <= c)
    return STARTS[a] + a % 8 + c - CANON[a]


def windows(features, nh):
    wide = features // nh
    ends = [(padded_column(k * wide), padded_column(k * wide + wide - 1)) for k in range(nh)]
    starts = [lo // 16 * 16 for lo, _ in ends]
    width = max(-(-(hi + 1 - lo) // 128) * 128 for lo, (_, hi) in zip(starts, ends))
    starts = [min(lo, PADDED - width) for lo in starts]
    assert starts[0] == 0 and all(b - a <= width for a, b in zip(starts, starts[1:]))
    return starts, width


def joined(landed, starts):
    ends = starts[1:] + [PADDED]
    return jnp.concatenate(
        [landed[k].T[: ends[k] - starts[k]] for k in range(len(starts))], axis=0
    )


def window_at(starts, owner, nh):
    at = starts[0]
    for k in range(1, nh):
        at = at + (starts[k] - starts[k - 1]) * ((owner + nh - k) // nh)
    return at


def masked(full, causal):
    n = full.shape[0]
    last = jnp.where(causal, full[n - CHUNK :], 0.0)
    if n == CHUNK:
        return last.astype(BF16)
    return jnp.concatenate([full[: n - CHUNK], last], axis=0).astype(BF16)


def main_kernel(ns, nh, names, starts, width, *refs):
    r = dict(zip(names, refs))
    q_ref, kv_ref, init_ref, og_ref = r["q"], r["kv"], r["init"], r["og"]
    kvt, xs, x, row, df, f_all = r["kvt"], r["xs"], r["x"], r["row"], r["df"], r["f"]
    qt, ogt, attt, qgt, dnt = r["qt"], r["ogt"], r["attt"], r["qgt"], r["dnt"]
    startt, keys, vals, kt, vt = r["startt"], r["keys"], r["vals"], r["kt"], r["vt"]
    kvl = r["kvl"]
    padt, tall = r["padt"], r["tall"]
    tokens = q_ref.shape[0]
    heads = q_ref.shape[1] // HEAD_DIM
    chunks = tokens // CHUNK
    features = init_ref.shape[1]
    s, h, beside, peers = places(ns, nh)
    links = Links(r["sends"], r["recvs"])
    sems = lambda name: [r[name + x] for x in ("is", "ir", "os", "or", "ss", "sr") if name + x in r]
    early = Exchange(ns, nh, s, h, beside, 1, r["inbox"], r["outbox"], r["carry"], sems("a"))
    late = Exchange(ns, nh, s, h, beside, nh // 2, r["sinbox"], r["soutbox"], r["later"], sems("c"))
    loads = [
        pltpu.make_async_copy(r[name], r[name + "_in"], r["loads"].at[i])
        for i, name in enumerate(("q", "init", "og"))
    ]
    for load in loads:
        load.start()
    barrier = pltpu.get_barrier_semaphore()
    for device in peers:
        pl.semaphore_signal(barrier, inc=1, device_id=device, device_id_type=MESH)

    kvt[...] = kv_ref[...].astype(F32).T
    vt[...] = kvt[HEAD_DIM:, :].astype(BF16)
    u_ref = r["u"]
    for c in range(chunks):
        at = slice(c * CHUNK, (c + 1) * CHUNK)
        xs[...] = scaled(kvt[:HEAD_DIM, at])
        for k in range(nh):
            @pl.when(h == k)
            def _(c=c, at=at, k=k):
                write_window(kvt.at[:HEAD_DIM, at], xs, f_all.at[c], CHUNK, starts[k], width)
    u_ref[...] = sum(
        dot(vt[:, c * CHUNK : (c + 1) * CHUNK], f_all[c, :width, :], ((1,), (1,)))
        for c in range(chunks)
    )
    pl.semaphore_wait(barrier, len(peers))
    early.start_in(u_ref)
    for load in loads:
        load.wait()

    qt[...] = r["q_in"][...].astype(F32).T
    kt[...] = kvt[:HEAD_DIM, :].astype(BF16)
    keys[...] = kv_ref[:, :HEAD_DIM]
    vals[...] = kv_ref[:, HEAD_DIM:]
    causal = lax.broadcasted_iota(jnp.int32, (CHUNK, CHUNK), 0) <= lax.broadcasted_iota(
        jnp.int32, (CHUNK, CHUNK), 1
    )

    def inner(c):
        n = (c + 1) * CHUNK
        at = slice(c * CHUNK, n)

        def one_head(k, _):
            here = pl.ds(pl.multiple_of(k * HEAD_DIM, HEAD_DIM), HEAD_DIM)
            query = qt[here, at]
            x[...] = query
            xs[...] = scaled(query)
            write_features(x, xs, f_all.at[c * heads + k], CHUNK)
            logits = dot(keys[:n], query.astype(BF16))
            weights = masked(logits * logits * (1.0 / HEAD_DIM), causal)
            r[f"logits{c}"][k] = logits
            r[f"weights{c}"][k] = weights
            attt[here, at] = dot(vt[:, :n], weights)
            return 0

        lax.fori_loop(0, heads, one_head, 0)

    def upward(c):
        n = (c + 1) * CHUNK
        at = slice(c * CHUNK, n)

        def one_head(k, _):
            here = pl.ds(pl.multiple_of(k * HEAD_DIM, HEAD_DIM), HEAD_DIM)
            query = qt[here, at]
            xs[...] = scaled(query)
            dn = dnt[here, at]
            df[...] = dot(startt[...], dn)
            dw = dot(vals[:n], dn)
            dl = masked(dw * r[f"logits{c}"][k] * (2.0 / HEAD_DIM), causal)
            qgt[here, at] = dot(kt[:, :n], dl) + feature_grad(xs, df, row, CHUNK)
            kvl[:n, :HEAD_DIM] += dot(dl, query.astype(BF16), ((1,), (1,)))
            kvl[:n, HEAD_DIM:] += dot(r[f"weights{c}"][k], dn, ((1,), (1,)))
            return 0

        lax.fori_loop(0, heads, one_head, 0, unroll=True)

    wide = r["wide"]
    whole_lanes = features // 128 * 128
    padt[...] = jnp.zeros_like(padt)
    wide[:, whole_lanes:] = jnp.zeros_like(wide[:, whole_lanes:])
    wide[:, :features] = r["init_in"][...]
    tall[...] = wide[...].T
    for a in range(HEAD_DIM):
        at = STARTS[a] + a % 8
        padt[at : at + HEAD_DIM - a, :] = tall[CANON[a] : CANON[a] + HEAD_DIM - a, :]
    sgw = r["sgw"]
    for k in range(nh):
        sgw[k] = padt[starts[k] : starts[k] + width, :].T
    ogt[...] = r["og_in"][...].astype(F32).T
    order = list(range(chunks))
    for c in order[:1:-1]:
        inner(c)

    def prefixes():
        early.wait_in()
        total = jnp.zeros_like(r["inbox"][0])
        for m in range(ns):
            r["outbox"][m] = total
            total = total + r["inbox"][m]
        early.start_out()

    early.own(prefixes)
    for c in order[1::-1]:
        inner(c)
    pairs = range(nh // 2)
    ends = starts[1:] + [PADDED]
    lane = lax.broadcasted_iota(jnp.int32, (HEAD_DIM, width), 1)

    def size_of(window):
        at = window_at(starts, window, nh)
        return window_at(ends, window, nh) - at

    def rows_of(window):
        return pl.ds(pl.multiple_of(window_at(starts, window, nh), 16), width)

    low = r["low"]

    def read_window(window):
        state = sgw[window] + r["carry"][window]
        low[...] = jnp.where(lane < size_of(window), state, 0.0).astype(BF16)

    def partial(window):
        read_window(window)
        rows = rows_of(window)
        for c in range(chunks):
            for k in range(heads):
                here = slice(k * HEAD_DIM, (k + 1) * HEAD_DIM)
                at = slice(c * CHUNK, (c + 1) * CHUNK)
                attt[here, at] += dot(low[...], f_all[c * heads + k, rows, :])

    for i in pairs:
        early.wait_out(i)
        early.side_copy(i, h).start()
        partial(lax.rem(h + 2 * i, nh))
    for i in pairs:
        early.side_copy(i, beside).wait_recv()
        if i < pairs[-1]:
            partial(lax.rem(beside + 2 * i, nh))
    last = lax.rem(beside + 2 * pairs[-1], nh)
    read_window(last)

    def normalize(c, _):
        at = pl.ds(pl.multiple_of(c * CHUNK, CHUNK), CHUNK)
        for k in range(heads):
            here = slice(k * HEAD_DIM, (k + 1) * HEAD_DIM)
            numer = attt[here, at] + dot(low[...], f_all[c * heads + k, rows_of(last), :])
            scale = lax.rsqrt(jnp.mean(numer * numer, axis=0, keepdims=True) + EPS)
            normed = numer * scale
            up = ogt[here, at]
            attt[here, at] = normed
            dn = (scale * (up - normed * jnp.mean(up * normed, axis=0, keepdims=True))).astype(BF16)
            dnt[here, at] = dn
        return 0

    lax.fori_loop(0, chunks, normalize, 0, unroll=True)

    near = r["near"]

    def state_window(window):
        rows = rows_of(window)
        sgw[window] = sum(
            dot(
                f_all[c * heads + k, rows, :],
                dnt[k * HEAD_DIM : (k + 1) * HEAD_DIM, c * CHUNK : (c + 1) * CHUNK],
                ((1,), (1,)),
            )
            for c in range(chunks)
            for k in range(heads)
        ).T

    def swap(i, head):
        window = lax.rem(head + 2 * i, nh)
        return push(
            sgw.at[window], near.at[window // 2], r["ns"].at[window // 2],
            r["nr"].at[window // 2], (s, beside),
        )

    mids = [r["mid"].at[i] for i in pairs]
    for i in pairs[::-1]:
        state_window(lax.rem(beside + 2 * i, nh))
        swap(i, beside).start()
    for i in pairs[::-1]:
        window = lax.rem(h + 2 * i, nh)
        state_window(window)
        swap(i, h).wait_recv()
        r["mid"][i] = sgw[window] + near[window // 2]
        late.start_in(mids[i], i)
    early.end_in([u_ref])
    early.own(early.end_out)
    for i in pairs:
        early.side_copy(i, h).wait_send()
    startt[...] = (padt[...] + joined(r["carry"], starts)).astype(BF16)
    kvl[...] = jnp.zeros_like(kvl)
    for c in order[:1:-1]:
        upward(c)
    core = lax.rem(h, 2)
    kvnear, kvfar, kvsum = r["kvnear"], r["kvfar"], r["kvsum"]

    def kv_swap(q, side):
        return push(
            kvl.at[block(2 * q + side, CHUNK), :], kvnear.at[q], r["kvs"].at[q], r["kvr"].at[q], (s, beside)
        )

    kv_swap(1, 1 - core).start()
    tot, win = r["tot"], r["win"]

    def total_copies():
        return [
            push(
                tot, win.at[block(late.rank, 8), :], r["ts"].at[k], r["tr"].at[late.rank],
                (lax.rem(s + k, ns), h),
            )
            for k in range(1, ns)
        ]

    def suffixes():
        late.wait_in()
        total = jnp.zeros_like(r["sinbox"][0])
        for m in reversed(range(ns)):
            r["soutbox"][m] = total
            for i in pairs:
                total = total + r["sinbox"][m * (nh // 2) + i]
        tot[...] = total
        late.start_out()
        for copy in total_copies():
            copy.start()
        win[block(late.rank, 8), :] = total

    late.own(suffixes)
    upward(1)
    kvacross = []

    def kv_across(q):
        kv_swap(q, 1 - core).wait()
        kvsum[q] = kvl[block(2 * q + core, CHUNK), :] + kvnear[q]
        for k in range(1, nh // 2):
            to = (s, lax.rem(h + 2 * k, nh))
            kvacross.append(links.copy(kvsum.at[q], kvfar.at[k - 1, q], to))
            kvacross[-1].start()

    kv_across(1)
    upward(0)
    kv_swap(0, 1 - core).start()
    kxs = r["kxs"]
    for c in range(chunks):
        at = slice(c * CHUNK, (c + 1) * CHUNK)
        kxs[c] = scaled(kvt[:HEAD_DIM, at])
        write_features(kvt.at[:HEAD_DIM, at], kxs.at[c], f_all.at[c], CHUNK)
    kv_across(0)
    att_ref, qg_ref = r["att"], r["qg"]
    att_ref[...] = attt[...].T.astype(BF16)
    qg_ref[...] = qgt[...].T.astype(BF16)
    for i in pairs:
        swap(i, beside).wait_send()
    part_ref, other_ref, kv_out = r["part"], r["other"], r["kv_grad"]

    def chunk_of(k, side):
        return 2 * (k % (chunks // 2)) + (1 - side if k < chunks // 2 else side)

    def side(k):
        c = chunk_of(k, core)
        return push(
            part_ref.at[c], other_ref.at[c], r["xs_send"].at[c], r["xs_recv"].at[c], (s, beside)
        )

    def key_chunk(k, w, first):
        c = chunk_of(k, core)
        at = pl.ds(pl.multiple_of(c * CHUNK, CHUNK), CHUNK)
        size = ends[w] - starts[w]
        df[starts[w] : ends[w], :] = dot(startt[starts[w] : ends[w], :], vt[:, at])
        seen = dot(low[...], f_all[c, starts[w] : starts[w] + width, :])
        ranges = [(starts[w], ends[w])]
        grad = jnp.concatenate([feature_grad(kxs.at[c], df, row, CHUNK, ranges), seen], axis=0).T
        part_ref[c] = grad if first else part_ref[c] + grad

    for i in pairs:
        late.wait_out(i)
        for w in range(nh):
            @pl.when(lax.rem(h + 2 * i, nh) == w)
            def _(i=i, w=w):
                size = ends[w] - starts[w]
                state = r["later"][w]
                startt[starts[w] : ends[w], :] = state.T[:size].astype(BF16)
                low[...] = jnp.where(lane < size, state, 0.0).astype(BF16)
                for k in range(chunks):
                    if i == pairs[-1] and k == chunks // 2:
                        for copy in kvacross:
                            copy.wait()
                        for far in range(nh // 2 - 1):
                            kvsum[...] += kvfar[far]
                    key_chunk(k, w, i == 0)
                    if i == pairs[-1]:
                        if k >= chunks // 2:
                            part_ref[chunk_of(k, core)] += kvsum[k - chunks // 2]
                        side(k).start()
    late.end_in(mids)
    late.own(late.end_out)
    for k in range(late.groups):
        j = lax.rem(late.rank + k, late.groups)
        box = win.at[block(j, 8), :]
        copy = push(box, box, r["ts"].at[0], r["tr"].at[j], (s, beside))
        if k == 0:
            late.own(lambda: None, copy.wait_recv)
        else:
            copy.wait_recv()

    def end_totals():
        for copy in total_copies():
            copy.wait_send()

    late.own(end_totals)
    own_window = pl.ds(pl.multiple_of(window_at(starts, h, nh), 16), width)
    padt[own_window, :] = win[...].T
    canon = r["tall"]
    for a in range(HEAD_DIM):
        at = STARTS[a] + a % 8
        canon[CANON[a] : CANON[a] + HEAD_DIM - a, :] = padt[at : at + HEAD_DIM - a, :]
    slice_width = features // nh
    flip, init_out = r["flip"], r["init_grad"]
    flip[:slice_width, :] = canon[block(h, slice_width), :]
    init_out[...] = flip[...].T[:, :slice_width]
    for k in range(chunks):
        side(k).wait_send()
        c = chunk_of(k, 1 - core)
        copy = push(
            part_ref.at[c], other_ref.at[c], r["xs_send"].at[c], r["xs_recv"].at[c], (s, beside)
        )
        copy.wait_recv()
        kv_out[block(c, CHUNK), :] = part_ref[c] + other_ref[c]


def deliver_kernel(count, *refs):
    sems = refs[2 * count]
    copies = [
        pltpu.make_async_copy(refs[i], refs[count + i], sems.at[i]) for i in range(count)
    ]
    for copy in copies:
        copy.start()
    for copy in copies:
        copy.wait()


def deliver(arrays):
    here = pl.BlockSpec(memory_space=pl.ANY)
    return pl.pallas_call(
        functools.partial(deliver_kernel, len(arrays)),
        out_shape=tuple(jax.ShapeDtypeStruct(x.shape, x.dtype) for x in arrays),
        in_specs=[pl.BlockSpec(memory_space=pltpu.VMEM)] * len(arrays),
        out_specs=(here,) * len(arrays),
        scratch_shapes=[pltpu.SemaphoreType.DMA((len(arrays),))],
        compiler_params=pltpu.CompilerParams(vmem_limit_bytes=2 * 1024 * 1024),
    )(*arrays)


def per_device(ns, nh, queries, keys_values, init_state, out_grad):
    tokens, wide = queries.shape
    assert tokens == GROUP and ns % 8 == 0 and nh % 2 == 0 and tokens // nh == CHUNK
    features = init_state.shape[1]
    heads = wide // HEAD_DIM
    pair, groups = nh // 2, HEAD_DIM // 8
    even = -(-features // 128) * 128
    starts, width = windows(features, nh)
    slice_width = features // nh
    D, V = pltpu.SemaphoreType.DMA, pltpu.VMEM
    piece, window = (8, width), (HEAD_DIM, width)
    columns, chunk = (wide, tokens), (HEAD_DIM, CHUNK)
    count = 2 * (pair - 1)
    outs = dict(
        att=((tokens, wide), BF16),
        qg=((tokens, wide), BF16),
        kv_grad=((tokens, 2 * HEAD_DIM), F32),
        init_grad=((HEAD_DIM, slice_width), F32),
    )
    scratch = dict(
        q_in=V(queries.shape, BF16), init_in=V(init_state.shape, F32), og_in=V(out_grad.shape, BF16),
        loads=D((3,)), kvt=V((2 * HEAD_DIM, tokens), F32), x=V(chunk, F32), xs=V(chunk, F32), row=V(chunk, F32),
        df=V((PADDED, CHUNK), F32), f=V((tokens // CHUNK * heads, PADDED, CHUNK), BF16),
        qt=V(columns, F32), ogt=V(columns, F32), attt=V(columns, F32), qgt=V(columns, F32),
        dnt=V(columns, BF16), startt=V((PADDED, HEAD_DIM), BF16),
        keys=V((tokens, HEAD_DIM), BF16), vals=V((tokens, HEAD_DIM), BF16),
        kt=V((HEAD_DIM, tokens), BF16), vt=V((HEAD_DIM, tokens), BF16),
        carry=V((nh,) + window, F32), later=V((nh,) + window, F32),
        kvl=V((tokens, 2 * HEAD_DIM), F32), padt=V((PADDED, HEAD_DIM), F32),
        tall=V((even, HEAD_DIM), F32), wide=V((HEAD_DIM, even), F32),
        u=V(window, F32), inbox=V((ns,) + piece, F32), outbox=V((ns,) + piece, F32),
        sinbox=V((ns * pair,) + piece, F32), soutbox=V((ns,) + piece, F32), tot=V(piece, F32),
        near=V((pair,) + window, F32), mid=V((pair,) + window, F32), sgw=V((nh,) + window, F32),
        kvnear=V((2, CHUNK, 2 * HEAD_DIM), F32), kvsum=V((2, CHUNK, 2 * HEAD_DIM), F32),
        kvfar=V((max(pair - 1, 1), 2, CHUNK, 2 * HEAD_DIM), F32),
        kxs=V((tokens // CHUNK,) + chunk, F32), win=V(window, F32),
        part=V((tokens // CHUNK, CHUNK, 2 * HEAD_DIM), F32),
        other=V((tokens // CHUNK, CHUNK, 2 * HEAD_DIM), F32),
        flip=V((-(-slice_width // 128) * 128, HEAD_DIM), F32),
        xs_send=D((tokens // CHUNK,)), xs_recv=D((tokens // CHUNK,)), kvs=D((2,)), kvr=D((2,)), low=V((HEAD_DIM, width), BF16),
        sends=D((count,)), recvs=D((count,)), ns=D((pair,)), nr=D((pair,)), ts=D((ns,)), tr=D((groups,)),
        ais=D((groups,)), air=D((ns,)), cis=D((groups * pair,)), cir=D((ns * pair,)),
    )
    scratch["ass"], scratch["asr"] = D((pair,)), D((pair,))
    for name in ("a", "c"):
        scratch[name + "os"], scratch[name + "or"] = D((ns * pair,)), D((groups * pair,))
    for c in range(tokens // CHUNK):
        scratch[f"logits{c}"] = V((heads, (c + 1) * CHUNK, CHUNK), F32)
        scratch[f"weights{c}"] = V((heads, (c + 1) * CHUNK, CHUNK), BF16)
    names = ["q", "kv", "init", "og"] + list(outs) + list(scratch)
    vmem, far = pl.BlockSpec(memory_space=pltpu.VMEM), pl.BlockSpec(memory_space=pltpu.HBM)
    results = pl.pallas_call(
        functools.partial(main_kernel, ns, nh, names, starts, width),
        out_shape=tuple(pltpu.VMEM(*out) for out in outs.values()),
        in_specs=[far, vmem, far, far],
        out_specs=(vmem,) * len(outs),
        scratch_shapes=list(scratch.values()),
        compiler_params=pltpu.CompilerParams(
            vmem_limit_bytes=60 * 1024 * 1024, collective_id=1, has_side_effects=True
        ),
    )(queries, keys_values, init_state, out_grad)
    return deliver(results)


def solution(mesh):
    ns, nh = mesh.shape["seq"], mesh.shape["head"]
    return jax.shard_map(
        functools.partial(per_device, ns, nh),
        mesh=mesh,
        in_specs=(P("seq", "head"), P("seq", None), P(), P("seq", "head")),
        out_specs=(P("seq", "head"), P("seq", "head"), P("seq", None), P(None, "head")),
        check_vma=False,
    )
```
